256 devices in a mesh: seq: 32 (over y, z), expert: 8 (over x, core).
Axes of the slice: x: 4, y: 4, z: 8, core: 2. Of those that a mesh axis runs over, the one named last changes fastest.
Arguments:
- grad_out: bfloat16 [32768, 2048], P(('seq', 'expert')), may hold values from -6 to 6
- expert_input: bfloat16 [32768, 2048], P(('seq', 'expert')), may hold values from -6 to 6
- expert_index: int32 [32768, 2], P(('seq', 'expert')), may hold values from 0 to 7, all different within a row; in each aligned block of 128 rows (0 to 127, 128 to 255, ...) at most 64 rows name the same one
- route_weight: float32 [32768, 2], P(('seq', 'expert')), may hold values from 0.1 to 1
- up_weight: bfloat16 [8, 2048, 768], P('expert'), may hold values from -0.125 to 0.125
- down_weight: bfloat16 [8, 768, 2048], P('expert'), may hold values from -0.21875 to 0.21875
- out_weight: bfloat16 [4096, 2048], P('expert'), may hold values from -0.125 to 0.125
- conv_value: bfloat16 [32768, 4096], P('seq', 'expert'), may hold values from -6 to 6
- conv_weight: float32 [4, 4096], P(None, 'expert'), may hold values from -3 to 3
- step_size: float32 [64, 32768], P('expert', 'seq'), may hold values from 0.25 to 1
- log_decay: float32 [64, 32768], P('expert', 'seq'), may hold values from -1 to 0
- skip_gain: float32 [64], P('expert'), may hold values from 0.2 to 0.6
- input_basis: bfloat16 [32768, 1024], P('seq', 'expert'), may hold values from -0.09375 to 0.09375
- output_basis: bfloat16 [32768, 1024], P('seq', 'expert'), may hold values from -0.09375 to 0.09375
Outputs:
- residual_grad: bfloat16 [32768, 2048], P(('seq', 'expert'))
- conv_grad: bfloat16 [32768, 4096], P('seq', 'expert')
- input_basis_grad: bfloat16 [32768, 1024], P('seq', 'expert')
- output_basis_grad: bfloat16 [32768, 1024], P('seq', 'expert')
The draws below stay inside these ranges and needn't reach their ends.
Inputs may be any that keep to these rules, and one draw needn't show every extreme that they name: `expert_index`: in each aligned block of 128 rows (the rows of one device), no expert is named by more than 64 rows, and the 2 experts of a row differ.
All inputs are finite; a program needn't handle non-finite values.
Results may differ from the reference program's by a relative error of at most 0.01.
Values may be sent and summed in bfloat16 or wider, within the bound.
A program may use at most 128 MiB of HBM per device.

```python
import math
import jax
import jax.numpy as jnp
import numpy as np
from jax import lax

D = 2048
FF = 768
HALF_HEADS = 64
P_SIZE = 64
N = 128
GROUPS = 8
KW = 4
SPAN = 128
TOPK = 2
TOK_SEQ = 1024
TOK_DEV = 128
TOKEN_TOTAL = 32768
EXPERTS = 8
CH = 4096
CAP = 64


def draw_log_decay(key, part):
    random_keys = jax.random.split(key, 7)
    keep_share = 0.5
    block_total = TOKEN_TOTAL // TOK_SEQ
    slow_head = jax.random.uniform(random_keys[0], (HALF_HEADS, 1, 1), dtype=jnp.float32) < keep_share
    slow_rate = jnp.exp(jax.random.uniform(random_keys[1], (HALF_HEADS, 1, 1), dtype=jnp.float32, minval=math.log(0.5 / TOK_SEQ), maxval=math.log(4.0 / TOK_SEQ)))
    fast_rate = jnp.exp(jax.random.uniform(random_keys[2], (HALF_HEADS, 1, 1), dtype=jnp.float32, minval=math.log(1.0 / 50.0), maxval=math.log(1.0 / 30.0)))
    head_rate = jnp.where(slow_head, slow_rate, fast_rate)
    block_factor = jnp.exp(jax.random.uniform(random_keys[3], (HALF_HEADS, block_total, 1), dtype=jnp.float32, minval=math.log(0.5), maxval=math.log(2.0)))
    jitter = jax.random.uniform(random_keys[4], (HALF_HEADS, block_total, TOK_SEQ), dtype=jnp.float32, minval=0.5, maxval=1.5)
    drawn_tokens = -(head_rate * block_factor * jitter).reshape(HALF_HEADS, TOKEN_TOTAL)
    spike_places = jax.random.randint(random_keys[5], (2,), 0, TOKEN_TOTAL)
    token_positions = jnp.arange(TOKEN_TOTAL)
    spike_mask = jnp.any(token_positions[None, :] == spike_places[:, None], axis=0)
    spike_loss = jax.random.uniform(random_keys[6], (HALF_HEADS, TOKEN_TOTAL), dtype=jnp.float32, minval=0.2, maxval=0.5)
    return jnp.where(spike_mask[None, :], drawn_tokens + jnp.log(1.0 - spike_loss), drawn_tokens).astype(jnp.float32)


def steps_of(stream_key, shape, cuts, least, top_value):
    loudness = 1.0
    for axis_at, blocks in cuts:
        heights = jax.random.uniform(jax.random.fold_in(jax.random.fold_in(stream_key, 6), axis_at), (blocks,), jnp.float32, least / len(cuts), top_value / len(cuts))
        loudness = loudness * jnp.repeat(jnp.exp(heights), shape[axis_at] // blocks).reshape((-1,) + (1,) * (len(shape) - 1 - axis_at))
    return loudness


def routed_block(rng, own, number, rows, amount, top, bound, skew):
    order = jax.random.permutation(rng, amount)
    packed, usual = portions_of(amount, rows * top, bound, skew, True), portions_of(amount, rows * top, bound, skew, False)
    places = jnp.arange(amount)

    def named(lengths, turn):
        used = int((lengths > 0).sum())
        fixed = max(1, used // 4)
        shifted = fixed + (places - fixed + turn * (used - fixed)) % max(1, amount - fixed)
        return jnp.zeros((amount,), jnp.int32).at[order[jnp.where(places < fixed, places, shifted)]].set(jnp.asarray(lengths, jnp.int32))

    lengths = jnp.where(number % 4 == 0, named(packed, number // 4), named(usual, number - number // 4 - 1))
    mixed = jax.random.permutation(jax.random.fold_in(own, 3), amount)
    source_of, taker = mixed[0:amount // 2 * 2:2], mixed[1:amount // 2 * 2:2]
    margin = jnp.minimum(lengths[source_of] - 1, bound - lengths[taker]) // 2
    margin = jnp.where((source_of == order[0]) | (taker == order[0]) | (lengths[taker] == 0), 0, jnp.maximum(margin, 0))
    shifted = jax.random.randint(jax.random.fold_in(own, 4), (amount // 2,), 0, 1 << 20) % (margin + 1)
    lengths = lengths.at[source_of].add(-shifted).at[taker].add(shifted)
    items = jnp.searchsorted(jnp.cumsum(lengths), jnp.arange(rows * top), side="right").astype(jnp.int32)
    table = items.reshape(top, rows).T
    table = table[jax.random.permutation(jax.random.fold_in(own, 1), rows)]
    turn = jax.random.randint(jax.random.fold_in(own, 2), (rows, 1), 0, top)
    return jnp.take_along_axis(table, (jnp.arange(top)[None, :] + turn) % top, axis=1)


def portions_of(amount, total, limit, slope, full):
    weights = [(1 << 20) // math.isqrt(grade ** slope) + 1 for grade in range(1, amount + 1)]
    largest = limit if full else min(limit, max(-(-total // amount), total * weights[0] // sum(weights)))
    least = 1 if total - largest >= amount - 1 else 0
    counts, rest = [largest] + [least] * (amount - 1), total - largest - least * (amount - 1)
    while rest > 0:
        movable = [i for i in range(1, amount) if counts[i] < largest] or [i for i in range(1, amount) if counts[i] < limit]
        pool, budget = sum([weights[i] for i in movable]), rest
        for i in movable:
            addition = min(limit - counts[i], max(1, budget * weights[i] // pool), rest)
            counts[i] = counts[i] + addition
            rest = rest - addition
    return np.array(counts)


def bell_draw(stream_key, dims, scale, bound, cuts=(), kind=jnp.bfloat16):
    factor_of = steps_of(stream_key, dims, cuts, -0.22, 0.18) if cuts else 1.0
    drawn = jax.random.normal(stream_key, dims, jnp.float32) * scale * factor_of
    return jnp.minimum(jnp.maximum(drawn, -bound), bound).astype(kind)


def setup_inputs(seed: int = 0) -> dict:
    streams_of = jax.random.split(jax.random.key(seed), 15)
    grad_out = bell_draw(streams_of[0], (TOKEN_TOTAL, D), 1.0, 6.0, ((0, 256),))
    expert_input = bell_draw(streams_of[1], (TOKEN_TOTAL, D), 1.0, 6.0, ((0, 256),))
    expert_index_keys = jax.random.split(jax.random.fold_in(streams_of[2], 1), TOKEN_TOTAL // TOK_DEV)
    expert_index_turns = jax.random.permutation(jax.random.fold_in(streams_of[2], 3), TOKEN_TOTAL // TOK_DEV)
    expert_index = jax.vmap(lambda own, number: routed_block(jax.random.fold_in(streams_of[2], 2), own, number, TOK_DEV, EXPERTS, TOPK, CAP, 2))(expert_index_keys, expert_index_turns).reshape((TOKEN_TOTAL, TOPK))
    route_weight = jnp.clip(0.1 + 0.9 * jax.random.uniform(streams_of[3], (TOKEN_TOTAL, TOPK), jnp.float32) ** steps_of(streams_of[3], (TOKEN_TOTAL, TOPK), ((0, 256),), -0.2, 0.2), 0.1, 1.0)
    up_weight = bell_draw(streams_of[4], (EXPERTS, D, FF), D ** -0.5, 0.125, ((0, 8),))
    down_weight = bell_draw(streams_of[5], (EXPERTS, FF, D), FF ** -0.5, 0.21875, ((0, 8),))
    out_weight = bell_draw(streams_of[6], (CH, D), D ** -0.5, 0.125, ((0, 8),))
    conv_value = bell_draw(streams_of[7], (TOKEN_TOTAL, CH), 1.0, 6.0, ((0, 32), (1, 8)))
    conv_weight = bell_draw(streams_of[8], (KW, CH), KW ** -0.5, 3.0, ((1, 8),), jnp.float32)
    step_size = jnp.clip(jnp.exp(math.log(1.0) - 1.3862944 * jax.random.uniform(streams_of[9], (HALF_HEADS, TOKEN_TOTAL), jnp.float32) ** steps_of(streams_of[9], (HALF_HEADS, TOKEN_TOTAL), ((0, 8), (1, 32)), -0.2, 0.2)), 0.25, 1.0)
    log_decay = draw_log_decay(jax.random.fold_in(streams_of[14], 71), 0)
    skip_gain = jnp.clip(0.2 + 0.400000021 * jax.random.uniform(streams_of[11], (HALF_HEADS,), jnp.float32) ** steps_of(streams_of[11], (HALF_HEADS,), ((0, 8),), -0.2, 0.2), 0.2, 0.6)
    input_basis = bell_draw(streams_of[12], (TOKEN_TOTAL, GROUPS * N), 0.006, 0.09375, ((0, 32), (1, 8)))
    output_basis = bell_draw(streams_of[13], (TOKEN_TOTAL, GROUPS * N), 0.006, 0.09375, ((0, 32), (1, 8)))
    return dict(grad_out=grad_out, expert_input=expert_input, expert_index=expert_index, route_weight=route_weight, up_weight=up_weight, down_weight=down_weight, out_weight=out_weight, conv_value=conv_value, conv_weight=conv_weight, step_size=step_size, log_decay=log_decay, skip_gain=skip_gain, input_basis=input_basis, output_basis=output_basis)


def slot_tables(block_index, block_weight, expert_count, capacity):
    flat_index = block_index.reshape(-1)
    onehot_table = (flat_index[:, None] == jnp.arange(expert_count, dtype=jnp.int32)[None, :]).astype(jnp.int32)
    earlier_count = (jnp.cumsum(onehot_table, axis=0) - onehot_table).astype(jnp.int32)
    slot_rank = lax.optimization_barrier(jnp.sum(earlier_count * onehot_table, axis=1)).astype(jnp.int32)
    slot_place = (flat_index * capacity + slot_rank).astype(jnp.int32)
    owner_row = (jnp.arange(flat_index.shape[0], dtype=jnp.int32) // block_index.shape[1]).astype(jnp.int32)
    slot_match = slot_place[:, None] == jnp.arange(expert_count * capacity, dtype=jnp.int32)[None, :]
    source_row = lax.optimization_barrier(jnp.sum(jnp.where(slot_match, owner_row[:, None], 0), axis=0)).astype(jnp.int32)
    slot_filled = jnp.any(slot_match, axis=0)
    slot_weight = lax.optimization_barrier(jnp.sum(jnp.where(slot_match, block_weight.reshape(-1)[:, None], 0.0), axis=0))
    return (slot_place, source_row, slot_filled, slot_weight)

def expert_rows(input_rows, grad_rows, up_matrix, down_matrix):
    hidden_pre = jnp.dot(input_rows, up_matrix, preferred_element_type=jnp.float32)
    hidden_back = jnp.dot(grad_rows, down_matrix.T, preferred_element_type=jnp.float32)
    inner_grad = (2.0 * jnp.maximum(hidden_pre, 0.0) * hidden_back).astype(jnp.bfloat16)
    return jnp.dot(inner_grad, up_matrix.T, preferred_element_type=jnp.float32).astype(jnp.bfloat16)

def silu_grad(values):
    sigmoid_value = jax.nn.sigmoid(values)
    return sigmoid_value + values * sigmoid_value * (1.0 - sigmoid_value)

def forward_terms(mixed_act, in_basis, step_blocks, decay_blocks):
    cumulative = jnp.cumsum(decay_blocks, axis=-1)
    in_scale = jnp.exp(cumulative[..., -1:] - cumulative) * step_blocks
    row_scale = jnp.transpose(in_scale, (2, 3, 0, 1))[..., None]
    mixed_weighted = (mixed_act.astype(jnp.float32) * row_scale).astype(jnp.bfloat16)
    local_end = jnp.einsum('kqgn,kqghp->ghknp', in_basis, mixed_weighted, preferred_element_type=jnp.float32)
    return (cumulative, in_scale, mixed_weighted, local_end, jnp.exp(cumulative[..., -1]))

def backward_terms(cumulative, out_grad, out_basis):
    row_scale = jnp.transpose(jnp.exp(cumulative), (2, 3, 0, 1))[..., None]
    grad_weighted = (out_grad.astype(jnp.float32) * row_scale).astype(jnp.bfloat16)
    local_start = jnp.einsum('kqgn,kqghp->ghknp', out_basis, grad_weighted, preferred_element_type=jnp.float32)
    return (grad_weighted, local_start)

def advance(state_now, pair_now):
    return (pair_now[0][..., None, None] * state_now + pair_now[1], state_now)

def chain_forward(block_decay, local_terms, initial):
    moved = (jnp.moveaxis(block_decay, 2, 0), jnp.moveaxis(local_terms, 2, 0))
    final, entering = lax.scan(advance, initial, moved)
    return (final, jnp.moveaxis(entering, 0, 2))

def chain_backward(block_decay, local_terms, initial):
    moved = (jnp.moveaxis(block_decay, 2, 0), jnp.moveaxis(local_terms, 2, 0))
    final, leaving = lax.scan(advance, initial, moved, reverse=True)
    return (final, jnp.moveaxis(leaving, 0, 2))

def block_grads(cumulative, in_scale, mixed_act, out_grad, in_basis, out_basis, mixed_weighted, grad_weighted, entering, leaving, step_blocks, skip_heads):
    block_len = cumulative.shape[-1]
    lower_mask = jnp.arange(block_len)[:, None] >= jnp.arange(block_len)[None, :]
    spread = jnp.where(lower_mask, cumulative[..., :, None] - cumulative[..., None, :], 0.0)
    decay_mask = jnp.where(lower_mask, jnp.exp(spread), 0.0)
    step_column = step_blocks[..., None, :]
    scores = jnp.einsum('kagn,kbgn->gkab', out_basis, in_basis, preferred_element_type=jnp.float32)
    weight_scores = (decay_mask * step_column * scores[:, None]).astype(jnp.bfloat16)
    grad_mixed = jnp.einsum('kaghp,kbghp->ghkab', out_grad, mixed_act, preferred_element_type=jnp.float32)
    weight_grad = (decay_mask * step_column * grad_mixed).astype(jnp.bfloat16)
    entering_low = entering.astype(jnp.bfloat16)
    leaving_low = leaving.astype(jnp.bfloat16)
    inner_term = jnp.einsum('ghkab,kaghp->kbghp', weight_scores, out_grad, preferred_element_type=jnp.float32)
    carried = jnp.einsum('kbgn,ghknp->kbghp', in_basis, leaving_low, preferred_element_type=jnp.float32)
    row_scale = jnp.transpose(in_scale, (2, 3, 0, 1))[..., None]
    mixed_grad = inner_term + row_scale * carried + skip_heads[None, None, :, :, None] * out_grad.astype(jnp.float32)
    in_basis_grad = jnp.einsum('ghkab,kagn->kbgn', weight_grad, out_basis, preferred_element_type=jnp.float32)
    in_basis_grad = in_basis_grad + jnp.einsum('kbghp,ghknp->kbgn', mixed_weighted, leaving_low, preferred_element_type=jnp.float32)
    out_basis_grad = jnp.einsum('kaghp,ghknp->kagn', grad_weighted, entering_low, preferred_element_type=jnp.float32)
    out_basis_grad = out_basis_grad + jnp.einsum('ghkab,kbgn->kagn', weight_grad, in_basis, preferred_element_type=jnp.float32)
    return (mixed_grad, in_basis_grad, out_basis_grad)

def filter_back(value_grad, filter_taps, after_rows):
    row_count = value_grad.shape[0]
    padded = jnp.concatenate([value_grad, after_rows], axis=0)
    summed = filter_taps[0] * value_grad
    for tap_index in range(1, filter_taps.shape[0]):
        summed = summed + filter_taps[tap_index] * padded[tap_index:tap_index + row_count]
    return summed

def reference(grad_out, expert_input, expert_index, route_weight, up_weight, down_weight, out_weight, conv_value, conv_weight, step_size, log_decay, skip_gain, input_basis, output_basis):
    block_total = TOKEN_TOTAL // TOK_DEV
    index_blocks = expert_index.reshape(block_total, TOK_DEV, TOPK)
    weight_blocks = route_weight.reshape(block_total, TOK_DEV, TOPK)
    slot_place, source_row, slot_filled, slot_weight = jax.vmap(lambda index_block, weight_block: slot_tables(index_block, weight_block, EXPERTS, CAP))(index_blocks, weight_blocks)
    row_offset = (jnp.arange(block_total, dtype=jnp.int32) * TOK_DEV)[:, None]
    rows_at = (source_row + row_offset).astype(jnp.int32).reshape(block_total, EXPERTS, CAP)
    filled_at = slot_filled.reshape(block_total, EXPERTS, CAP)
    weight_at = slot_weight.reshape(block_total, EXPERTS, CAP)

    def one_expert(running, expert_number):
        rows_here = lax.dynamic_index_in_dim(rows_at, expert_number, 1, keepdims=False).reshape(-1)
        live_here = lax.dynamic_index_in_dim(filled_at, expert_number, 1, keepdims=False).reshape(-1)
        scale_here = lax.dynamic_index_in_dim(weight_at, expert_number, 1, keepdims=False).reshape(-1)
        inputs_here = jnp.where(live_here[:, None], jnp.take(expert_input, rows_here, axis=0), jnp.zeros((), expert_input.dtype))
        grads_here = (jnp.take(grad_out, rows_here, axis=0).astype(jnp.float32) * scale_here[:, None]).astype(jnp.bfloat16)
        result = expert_rows(inputs_here, grads_here, up_weight[expert_number], down_weight[expert_number])
        return (running.at[rows_here].add(jnp.where(live_here[:, None], result.astype(jnp.float32), 0.0)), None)
    expert_total, _ = lax.scan(one_expert, jnp.zeros((TOKEN_TOTAL, D), jnp.float32), jnp.arange(EXPERTS, dtype=jnp.int32))
    residual_grad = (grad_out.astype(jnp.float32) + expert_total).astype(jnp.bfloat16)
    per_group = HALF_HEADS // GROUPS
    block_count = TOKEN_TOTAL // SPAN
    width_here = per_group * P_SIZE

    def one_group(group_number):
        head_start = group_number * per_group
        columns = head_start * P_SIZE
        pre_value = lax.dynamic_slice_in_dim(conv_value, columns, width_here, 1).astype(jnp.float32)
        mixed_act = jax.nn.silu(pre_value).astype(jnp.bfloat16).reshape(block_count, SPAN, 1, per_group, P_SIZE)
        out_rows = lax.dynamic_slice_in_dim(out_weight, columns, width_here, 0)
        out_grad = jnp.dot(residual_grad, out_rows.T, preferred_element_type=jnp.float32).astype(jnp.bfloat16)
        out_grad = out_grad.reshape(block_count, SPAN, 1, per_group, P_SIZE)
        in_basis = lax.dynamic_slice_in_dim(input_basis, group_number * N, N, 1).reshape(block_count, SPAN, 1, N)
        out_basis = lax.dynamic_slice_in_dim(output_basis, group_number * N, N, 1).reshape(block_count, SPAN, 1, N)
        step_blocks = lax.dynamic_slice_in_dim(step_size, head_start, per_group, 0).reshape(1, per_group, block_count, SPAN)
        decay_blocks = lax.dynamic_slice_in_dim(log_decay, head_start, per_group, 0).reshape(1, per_group, block_count, SPAN)
        skip_heads = lax.dynamic_slice_in_dim(skip_gain, head_start, per_group, 0).reshape(1, per_group)
        cumulative, in_scale, mixed_weighted, local_end, block_decay = forward_terms(mixed_act, in_basis, step_blocks, decay_blocks)
        grad_weighted, local_start = backward_terms(cumulative, out_grad, out_basis)
        zero_state = jnp.zeros((1, per_group, N, P_SIZE), jnp.float32)
        _, entering = chain_forward(block_decay, local_end, zero_state)
        _, leaving = chain_backward(block_decay, local_start, zero_state)
        mixed_grad, in_grad, out_part = block_grads(cumulative, in_scale, mixed_act, out_grad, in_basis, out_basis, mixed_weighted, grad_weighted, entering, leaving, step_blocks, skip_heads)
        value_grad = mixed_grad.reshape(TOKEN_TOTAL, width_here) * silu_grad(pre_value)
        filter_taps = lax.dynamic_slice_in_dim(conv_weight, columns, width_here, 1)
        group_conv = filter_back(value_grad, filter_taps, jnp.zeros((KW - 1, width_here), jnp.float32)).astype(jnp.bfloat16)
        return (group_conv, in_grad.reshape(TOKEN_TOTAL, N).astype(jnp.bfloat16), out_part.reshape(TOKEN_TOTAL, N).astype(jnp.bfloat16))
    conv_parts, in_parts, out_parts = lax.map(one_group, jnp.arange(GROUPS, dtype=jnp.int32))
    conv_grad = jnp.transpose(conv_parts, (1, 0, 2)).reshape(TOKEN_TOTAL, CH)
    input_basis_grad = jnp.transpose(in_parts, (1, 0, 2)).reshape(TOKEN_TOTAL, GROUPS * N)
    output_basis_grad = jnp.transpose(out_parts, (1, 0, 2)).reshape(TOKEN_TOTAL, GROUPS * N)
    return (residual_grad, conv_grad, input_basis_grad, output_basis_grad)
```

```python
import jax
import jax.numpy as jnp
from jax import lax
from jax.sharding import PartitionSpec as P

P_SIZE = 64
N = 128
KW = 4
SPAN = 128


def from_behind(value, axis, by):
    devices = lax.axis_size(axis)
    pairs = [(i, i + by) for i in range(devices) if 0 <= i + by < devices]
    return lax.ppermute(value, axis, pairs)


def slot_tables(block_index, block_weight, expert_count, capacity):
    flat_index = block_index.reshape(-1)
    onehot_table = (
        flat_index[:, None] == jnp.arange(expert_count, dtype=jnp.int32)[None, :]
    ).astype(jnp.int32)
    earlier_count = jnp.cumsum(onehot_table, axis=0) - onehot_table
    slot_rank = jnp.sum(earlier_count * onehot_table, axis=1)
    slot_place = flat_index * capacity + slot_rank
    owner_row = jnp.arange(flat_index.shape[0], dtype=jnp.int32) // block_index.shape[1]
    slot_match = (
        slot_place[:, None] == jnp.arange(expert_count * capacity, dtype=jnp.int32)[None, :]
    )
    source_row = jnp.sum(jnp.where(slot_match, owner_row[:, None], 0), axis=0)
    slot_filled = jnp.any(slot_match, axis=0)
    slot_weight = jnp.sum(jnp.where(slot_match, block_weight.reshape(-1)[:, None], 0.0), axis=0)
    return (slot_place, source_row, slot_filled, slot_weight)


def expert_rows(input_rows, grad_rows, up_matrix, down_matrix):
    hidden_pre = jnp.dot(input_rows, up_matrix, preferred_element_type=jnp.float32)
    hidden_back = jnp.dot(grad_rows, down_matrix.T, preferred_element_type=jnp.float32)
    inner_grad = (2.0 * jnp.maximum(hidden_pre, 0.0) * hidden_back).astype(jnp.bfloat16)
    return jnp.dot(inner_grad, up_matrix.T, preferred_element_type=jnp.float32).astype(jnp.bfloat16)


def combine_rows(grad_rows, slot_place, returned):
    row_count = grad_rows.shape[0]
    flat_rows = returned.reshape(-1, returned.shape[-1])
    picked = (
        jnp.take(flat_rows, slot_place, axis=0)
        .astype(jnp.float32)
        .reshape(row_count, -1, flat_rows.shape[-1])
    )
    return (grad_rows.astype(jnp.float32) + jnp.sum(picked, axis=1)).astype(jnp.bfloat16)


def silu_grad(values):
    sigmoid_value = jax.nn.sigmoid(values)
    return sigmoid_value + values * sigmoid_value * (1.0 - sigmoid_value)


def forward_terms(mixed_act, in_basis, step_blocks, decay_blocks):
    cumulative = jnp.cumsum(decay_blocks, axis=-1)
    in_scale = jnp.exp(cumulative[..., -1:] - cumulative) * step_blocks
    row_scale = jnp.transpose(in_scale, (2, 3, 0, 1))[..., None]
    mixed_weighted = (mixed_act.astype(jnp.float32) * row_scale).astype(jnp.bfloat16)
    local_end = jnp.einsum(
        "kqgn,kqghp->ghknp", in_basis, mixed_weighted, preferred_element_type=jnp.float32
    )
    return (cumulative, in_scale, mixed_weighted, local_end, jnp.exp(cumulative[..., -1]))


def backward_terms(cumulative, out_grad, out_basis):
    row_scale = jnp.transpose(jnp.exp(cumulative), (2, 3, 0, 1))[..., None]
    grad_weighted = (out_grad.astype(jnp.float32) * row_scale).astype(jnp.bfloat16)
    local_start = jnp.einsum(
        "kqgn,kqghp->ghknp", out_basis, grad_weighted, preferred_element_type=jnp.float32
    )
    return (grad_weighted, local_start)


def advance(state_now, pair_now):
    return (pair_now[0][..., None, None] * state_now + pair_now[1], state_now)


def chain_forward(block_decay, local_terms, initial):
    moved = (jnp.moveaxis(block_decay, 2, 0), jnp.moveaxis(local_terms, 2, 0))
    final, entering = lax.scan(advance, initial, moved)
    return (final, jnp.moveaxis(entering, 0, 2))


def chain_backward(block_decay, local_terms, initial):
    moved = (jnp.moveaxis(block_decay, 2, 0), jnp.moveaxis(local_terms, 2, 0))
    final, leaving = lax.scan(advance, initial, moved, reverse=True)
    return (final, jnp.moveaxis(leaving, 0, 2))


def block_grads(
    cumulative,
    in_scale,
    mixed_act,
    out_grad,
    in_basis,
    out_basis,
    mixed_weighted,
    grad_weighted,
    entering,
    leaving,
    step_blocks,
    skip_heads,
):
    block_len = cumulative.shape[-1]
    lower_mask = jnp.arange(block_len)[:, None] >= jnp.arange(block_len)[None, :]
    spread = jnp.where(lower_mask, cumulative[..., :, None] - cumulative[..., None, :], 0.0)
    decay_mask = jnp.where(lower_mask, jnp.exp(spread), 0.0)
    step_column = step_blocks[..., None, :]
    scores = jnp.einsum("kagn,kbgn->gkab", out_basis, in_basis, preferred_element_type=jnp.float32)
    weight_scores = (decay_mask * step_column * scores[:, None]).astype(jnp.bfloat16)
    grad_mixed = jnp.einsum(
        "kaghp,kbghp->ghkab", out_grad, mixed_act, preferred_element_type=jnp.float32
    )
    weight_grad = (decay_mask * step_column * grad_mixed).astype(jnp.bfloat16)
    entering_low = entering.astype(jnp.bfloat16)
    leaving_low = leaving.astype(jnp.bfloat16)
    inner_term = jnp.einsum(
        "ghkab,kaghp->kbghp", weight_scores, out_grad, preferred_element_type=jnp.float32
    )
    carried = jnp.einsum(
        "kbgn,ghknp->kbghp", in_basis, leaving_low, preferred_element_type=jnp.float32
    )
    row_scale = jnp.transpose(in_scale, (2, 3, 0, 1))[..., None]
    mixed_grad = (
        inner_term
        + row_scale * carried
        + skip_heads[None, None, :, :, None] * out_grad.astype(jnp.float32)
    )
    in_basis_grad = jnp.einsum(
        "ghkab,kagn->kbgn", weight_grad, out_basis, preferred_element_type=jnp.float32
    )
    in_basis_grad = in_basis_grad + jnp.einsum(
        "kbghp,ghknp->kbgn", mixed_weighted, leaving_low, preferred_element_type=jnp.float32
    )
    out_basis_grad = jnp.einsum(
        "kaghp,ghknp->kagn", grad_weighted, entering_low, preferred_element_type=jnp.float32
    )
    out_basis_grad = out_basis_grad + jnp.einsum(
        "ghkab,kbgn->kagn", weight_grad, in_basis, preferred_element_type=jnp.float32
    )
    return (mixed_grad, in_basis_grad, out_basis_grad)


def device_chain(device_decay, device_state, backward):
    devices = lax.axis_size("seq")
    shape = device_state.shape
    pieces = device_state.astype(jnp.bfloat16).reshape(devices, -1)
    arrived = lax.all_to_all(pieces, "seq", split_axis=0, concat_axis=0, tiled=True)
    decays = lax.all_gather(device_decay.reshape(-1), "seq", axis=0)
    head = lax.axis_index("seq") * decays.shape[1] // devices
    own_decay = lax.dynamic_index_in_dim(decays, head, 1, keepdims=False)
    running = jnp.zeros(arrived.shape[1:], jnp.float32)
    results = [None] * devices
    order = range(devices - 1, -1, -1) if backward else range(devices)
    for place in order:
        results[place] = running.astype(jnp.bfloat16)
        running = own_decay[place] * running + arrived[place].astype(jnp.float32)
    returned = lax.all_to_all(jnp.stack(results), "seq", split_axis=0, concat_axis=0, tiled=True)
    return returned.reshape(shape).astype(jnp.float32)


def filter_back(value_grad, filter_taps, after_rows):
    row_count = value_grad.shape[0]
    padded = jnp.concatenate([value_grad, after_rows], axis=0)
    summed = filter_taps[0] * value_grad
    for tap_index in range(1, filter_taps.shape[0]):
        summed = summed + filter_taps[tap_index] * padded[tap_index : tap_index + row_count]
    return summed


def shards(
    grad_out,
    expert_input,
    expert_index,
    route_weight,
    up_weight,
    down_weight,
    out_weight,
    conv_value,
    conv_weight,
    step_size,
    log_decay,
    skip_gain,
    input_basis,
    output_basis,
):
    expert_count = lax.axis_size("expert")
    row_count, choose_count = expert_index.shape
    capacity = 2 * row_count * choose_count // expert_count
    model_width = grad_out.shape[1]
    head_count, seq_length = step_size.shape
    group_count = input_basis.shape[1] // N
    per_group = head_count // group_count
    block_count = seq_length // SPAN
    pre_value = conv_value.astype(jnp.float32)
    mixed_act = (
        jax.nn.silu(pre_value)
        .astype(jnp.bfloat16)
        .reshape(block_count, SPAN, group_count, per_group, P_SIZE)
    )
    in_basis = input_basis.reshape(block_count, SPAN, group_count, N)
    out_basis = output_basis.reshape(block_count, SPAN, group_count, N)
    step_blocks = step_size.reshape(group_count, per_group, block_count, SPAN)
    decay_blocks = log_decay.reshape(group_count, per_group, block_count, SPAN)
    skip_heads = skip_gain.reshape(group_count, per_group)
    cumulative, in_scale, mixed_weighted, local_end, block_decay = forward_terms(
        mixed_act, in_basis, step_blocks, decay_blocks
    )
    zero_state = jnp.zeros((group_count, per_group, N, P_SIZE), jnp.float32)
    device_decay = jnp.exp(jnp.sum(cumulative[..., -1], axis=-1))
    device_state, _ = chain_forward(block_decay, local_end, zero_state)

    enter_state = device_chain(device_decay, device_state, False)
    _, entering = chain_forward(block_decay, local_end, enter_state)
    slot_place, source_row, slot_filled, slot_weight = slot_tables(
        expert_index, route_weight, expert_count, capacity
    )
    send_inputs = jnp.where(
        slot_filled[:, None],
        jnp.take(expert_input, source_row, axis=0),
        jnp.zeros((), expert_input.dtype),
    )
    send_grads = (
        jnp.take(grad_out, source_row, axis=0).astype(jnp.float32) * slot_weight[:, None]
    ).astype(jnp.bfloat16)
    send_inputs = send_inputs.reshape(expert_count, capacity, model_width)
    send_grads = send_grads.reshape(expert_count, capacity, model_width)
    up_local = up_weight[0]
    down_local = down_weight[0]
    arrived = (
        lax.all_to_all(send_inputs, "expert", split_axis=0, concat_axis=0, tiled=True),
        lax.all_to_all(send_grads, "expert", split_axis=0, concat_axis=0, tiled=True),
    )
    sender_count = arrived[0].shape[0]
    item_count = arrived[0].shape[1]
    result = expert_rows(
        arrived[0].reshape(sender_count * item_count, model_width),
        arrived[1].reshape(sender_count * item_count, model_width),
        up_local,
        down_local,
    )
    returned = lax.all_to_all(
        result.reshape(sender_count, item_count, model_width),
        "expert",
        split_axis=0,
        concat_axis=0,
        tiled=True,
    )
    residual_grad = combine_rows(grad_out, slot_place, returned)
    grad_rows = jnp.dot(
        lax.all_gather(residual_grad, "expert", axis=0, tiled=True),
        out_weight.T,
        preferred_element_type=jnp.float32,
    )
    out_grad = grad_rows.astype(jnp.bfloat16).reshape(
        block_count, SPAN, group_count, per_group, P_SIZE
    )
    grad_weighted, local_start = backward_terms(cumulative, out_grad, out_basis)
    device_grad, _ = chain_backward(block_decay, local_start, zero_state)

    leave_grad = device_chain(device_decay, device_grad, True)
    _, leaving = chain_backward(block_decay, local_start, leave_grad)
    mixed_grad, in_grad, out_part = block_grads(
        cumulative,
        in_scale,
        mixed_act,
        out_grad,
        in_basis,
        out_basis,
        mixed_weighted,
        grad_weighted,
        entering,
        leaving,
        step_blocks,
        skip_heads,
    )
    value_grad = mixed_grad.reshape(seq_length, head_count * P_SIZE) * silu_grad(pre_value)
    after_rows = from_behind(value_grad[: KW - 1], "seq", -1)
    conv_grad = filter_back(value_grad, conv_weight, after_rows).astype(jnp.bfloat16)
    input_basis_grad = in_grad.reshape(seq_length, group_count * N).astype(jnp.bfloat16)
    output_basis_grad = out_part.reshape(seq_length, group_count * N).astype(jnp.bfloat16)
    return (residual_grad, conv_grad, input_basis_grad, output_basis_grad)


def solution(mesh):
    in_specs = (
        P(("seq", "expert"), None),
        P(("seq", "expert"), None),
        P(("seq", "expert"), None),
        P(("seq", "expert"), None),
        P("expert", None, None),
        P("expert", None, None),
        P("expert", None),
        P("seq", "expert"),
        P(None, "expert"),
        P("expert", "seq"),
        P("expert", "seq"),
        P("expert"),
        P("seq", "expert"),
        P("seq", "expert"),
    )
    out_specs = (
        P(("seq", "expert"), None),
        P("seq", "expert"),
        P("seq", "expert"),
        P("seq", "expert"),
    )
    return jax.shard_map(shards, mesh=mesh, in_specs=in_specs, out_specs=out_specs, check_vma=False)
```

```python
import functools

import jax
import jax.numpy as jnp
from jax import lax
from jax.experimental import pallas as pl
from jax.experimental.pallas import tpu as pltpu
from jax.sharding import PartitionSpec as P

P_SIZE = 64
N = 128
KW = 4
SPAN = 128
LANES = 128
MESH = pl.DeviceIdType.MESH
F32 = jnp.float32
BF16 = jnp.bfloat16


def dot(a, b, left, right):
    return lax.dot_general(a, b, (((left,), (right,)), ((), ())), preferred_element_type=F32)


def expert_kernel(
    input_ref,
    grad_ref,
    route_ref,
    up_ref,
    down_ref,
    out_weight_ref,
    residual_ref,
    out_grad_ref,
    inputs,
    grads,
    partial,
    gathered,
    sibling_part,
    far_part,
    near_part,
    summed,
    routes,
    hidden,
    up,
    down,
    out_weight,
    local_sem,
    send_sem,
    recv_sem,
):
    me = lax.axis_index("expert")
    count = lax.axis_size("expert")
    chips = count // 2
    chip, core = me // 2, me % 2
    rows = input_ref.shape[0]
    half = rows // 2
    low, high, whole = pl.ds(0, half), pl.ds(half, half), pl.ds(0, rows)
    other, other_low, other_high = pl.ds(rows, rows), pl.ds(rows, half), pl.ds(rows + half, half)

    def device(chip_step, core_step):
        return ((chip + chip_step) % chips) * 2 + (core + core_step) % 2

    sibling, right, left = device(0, 1), device(1, 0), device(chips - 1, 0)
    copies = {}

    def send(name, source, target_ref, target):
        place = len(copies)
        copies[name] = pltpu.make_async_remote_copy(
            src_ref=source,
            dst_ref=target_ref,
            send_sem=send_sem.at[place],
            recv_sem=recv_sem.at[place],
            device_id={"expert": target},
            device_id_type=MESH,
        )
        copies[name].start()

    def arrived(*names):
        for name in names:
            copies[name].wait_recv()

    loads = []
    for place, (source, target) in enumerate(
        (
            (input_ref, inputs.at[0, whole]),
            (up_ref, up),
            (route_ref.at[me], routes.at[0]),
            (grad_ref, grads.at[0, whole]),
            (down_ref, down),
            (out_weight_ref, out_weight),
        )
    ):
        loads.append(pltpu.make_async_copy(source, target, local_sem.at[place]))
        loads[-1].start()

    barrier = pltpu.get_barrier_semaphore()
    for step in range(1, count):
        pl.semaphore_signal(
            barrier, inc=1, device_id={"expert": (me + step) % count}, device_id_type=MESH
        )
    pl.semaphore_wait(barrier, count - 1)

    def first(tag, source, buffer):
        send(tag + "r1", source.at[low], buffer.at[1, low], right)
        send(tag + "l1", source.at[high], buffer.at[2, high], left)
        send(tag + "s0", source, buffer.at[0, other], sibling)

    def second(tag, source, buffer):
        send(tag + "r2", source.at[high], buffer.at[1, high], right)
        send(tag + "l2", source.at[low], buffer.at[2, low], left)

    def forward(tag, buffer):
        arrived(tag + "r1")
        send(tag + "r3", buffer.at[1, low], buffer.at[3, low], right)
        send(tag + "s1", buffer.at[1, low], buffer.at[1, other_low], sibling)
        arrived(tag + "l1")
        send(tag + "l3", buffer.at[2, high], buffer.at[3, high], left)
        send(tag + "s2", buffer.at[2, high], buffer.at[2, other_high], sibling)

    def share_near(tag, buffer):
        arrived(tag + "r2")
        send(tag + "s3", buffer.at[1, high], buffer.at[1, other_high], sibling)
        arrived(tag + "l2")
        send(tag + "s4", buffer.at[2, low], buffer.at[2, other_low], sibling)

    def share_far(tag, buffer):
        arrived(tag + "r3")
        send(tag + "s5", buffer.at[3, low], buffer.at[3, other_low], sibling)
        arrived(tag + "l3")
        send(tag + "s6", buffer.at[3, high], buffer.at[3, other_high], sibling)

    first("x", input_ref, inputs)
    first("g", grad_ref, grads)
    for chip_step, slot in ((0, 0), (1, 1), (chips - 1, 2), (2, 3)):
        for core_step in range(2):
            if (chip_step, core_step) != (0, 0):
                target = device(chip_step, core_step)
                send(
                    "w%d%d" % (slot, core_step),
                    route_ref.at[target],
                    routes.at[2 * slot + core_step],
                    target,
                )
    second("x", input_ref, inputs)

    def before(slot):
        hidden[slot] = 2.0 * jnp.maximum(dot(inputs[slot], up[...], 1, 0), 0.0)

    def after(slot):
        column = jnp.concatenate(
            [routes[2 * slot].T[:, 0:1], routes[2 * slot + 1].T[:, 0:1]], axis=0
        )
        back = dot(grads[slot], down[...], 1, 1) * column
        inner = (hidden[slot] * back).astype(BF16)
        partial[slot] = dot(inner, up[...], 1, 1).astype(BF16)
        send("p%d" % slot, partial.at[slot, other], sibling_part.at[slot], sibling)

    loads[0].wait()
    loads[1].wait()
    arrived("xs0")
    before(0)
    forward("x", inputs)
    loads[2].wait()
    for slot, core_step in ((0, 1), (1, 0), (1, 1), (2, 0), (2, 1), (3, 0), (3, 1)):
        arrived("w%d%d" % (slot, core_step))
    loads[3].wait()
    loads[4].wait()
    forward("g", grads)
    second("g", grad_ref, grads)
    arrived("gs0")
    after(0)
    share_near("x", inputs)
    arrived("xs1", "xs3")
    before(1)
    arrived("xs2", "xs4")
    before(2)
    share_far("x", inputs)
    arrived("xs5", "xs6")
    before(3)
    share_far("g", grads)
    arrived("gs5", "gs6")
    after(3)
    share_near("g", grads)
    arrived("p3")
    summed[0] = partial[3, whole] + sibling_part[3]
    send("fr", summed.at[0, low], far_part.at[0], right)
    send("fl", summed.at[0, high], far_part.at[1], left)
    arrived("gs2", "gs4")
    after(2)
    arrived("gs1", "gs3")
    after(1)
    arrived("p2")
    summed[1, high] = partial[2, high] + sibling_part[2, high]
    send("nr1", summed.at[1, high], near_part.at[0, high], right)
    arrived("p1")
    summed[2, low] = partial[1, low] + sibling_part[1, low]
    send("nl1", summed.at[2, low], near_part.at[1, low], left)

    def three(a, b, c):
        return (a.astype(F32) + b.astype(F32) + c.astype(F32)).astype(BF16)

    arrived("fr")
    summed[1, low] = three(partial[2, low], sibling_part[2, low], far_part[0])
    send("nr2", summed.at[1, low], near_part.at[0, low], right)
    arrived("fl")
    summed[2, high] = three(partial[1, high], sibling_part[1, high], far_part[1])
    send("nl2", summed.at[2, high], near_part.at[1, high], left)
    loads[5].wait()
    arrived("p0")

    def finish(part):
        gathered[0, part] = (
            grads[0, part].astype(F32)
            + partial[0, part].astype(F32)
            + sibling_part[0, part].astype(F32)
            + near_part[0, part].astype(F32)
            + near_part[1, part].astype(F32)
        ).astype(BF16)

    arrived("nr1", "nl1", "nr2", "nl2")
    finish(low)
    finish(high)
    own = gathered.at[0, whole]
    first("o", own, gathered)
    second("o", own, gathered)
    store = pltpu.make_async_copy(own, residual_ref, local_sem.at[0])
    store.start()

    def project(slot, chip_step):
        product = dot(gathered[slot], out_weight[...], 1, 1).astype(BF16)
        for core_step in range(2):
            start = pl.multiple_of(device(chip_step, core_step) * rows, rows)
            out_grad_ref[pl.ds(start, rows)] = product[core_step * rows : (core_step + 1) * rows]

    forward("o", gathered)
    arrived("os0")
    project(0, 0)
    share_near("o", gathered)
    arrived("os1", "os3")
    project(1, chips - 1)
    arrived("os2", "os4")
    project(2, 1)
    share_far("o", gathered)
    arrived("os5", "os6")
    project(3, 2)
    store.wait()
    for copy in copies.values():
        copy.wait_send()


def expert_part(grad_out, expert_input, expert_index, route_weight, up, down, out_weight):
    count = lax.axis_size("expert")
    rows, width = grad_out.shape
    inner = up.shape[1]
    columns = out_weight.shape[0]
    match = expert_index[None] == jnp.arange(count, dtype=jnp.int32)[:, None, None]
    table = jnp.sum(jnp.where(match, route_weight[None], 0.0), axis=2)
    routes = jnp.broadcast_to(table[:, None, :], (count, 8, rows))
    copies = 64
    hbm = pl.BlockSpec(memory_space=pl.ANY)
    return pl.pallas_call(
        expert_kernel,
        out_shape=(
            jax.ShapeDtypeStruct((rows, width), BF16),
            jax.ShapeDtypeStruct((count * rows, columns), BF16),
        ),
        in_specs=[hbm] * 6,
        out_specs=(hbm, pl.BlockSpec(memory_space=pltpu.VMEM)),
        scratch_shapes=[
            pltpu.VMEM((4, 2 * rows, width), BF16),
            pltpu.VMEM((4, 2 * rows, width), BF16),
            pltpu.VMEM((4, 2 * rows, width), BF16),
            pltpu.VMEM((4, 2 * rows, width), BF16),
            pltpu.VMEM((4, rows, width), BF16),
            pltpu.VMEM((2, rows // 2, width), BF16),
            pltpu.VMEM((2, rows, width), BF16),
            pltpu.VMEM((3, rows, width), BF16),
            pltpu.VMEM((8, 8, rows), F32),
            pltpu.VMEM((4, 2 * rows, inner), F32),
            pltpu.VMEM((width, inner), BF16),
            pltpu.VMEM((inner, width), BF16),
            pltpu.VMEM((columns, width), BF16),
            pltpu.SemaphoreType.DMA((6,)),
            pltpu.SemaphoreType.DMA((copies,)),
            pltpu.SemaphoreType.DMA((copies,)),
        ],
        compiler_params=pltpu.CompilerParams(
            collective_id=1, has_side_effects=True, vmem_limit_bytes=60 * 1024 * 1024
        ),
        name="expert_part",
    )(expert_input, grad_out, routes, up, down, out_weight)


def widen(columns):
    lane = lax.broadcasted_iota(jnp.int32, (columns.shape[0], LANES), 1)
    parts = []
    for pair in range(columns.shape[1] // 2):
        one, two = columns[:, 2 * pair : 2 * pair + 1], columns[:, 2 * pair + 1 : 2 * pair + 2]
        parts.append(jnp.where(lane < P_SIZE, one, two))
    return jnp.concatenate(parts, axis=1)


def head_row(column, width):
    heads = column.shape[0]
    lane = lax.broadcasted_iota(jnp.int32, (heads, width), 1)
    head = lax.broadcasted_iota(jnp.int32, (heads, width), 0)
    chosen = jnp.where(lane // P_SIZE == head, column, 0.0)
    return jnp.broadcast_to(jnp.sum(chosen, axis=0, keepdims=True), (8, width))


def mixer_kernel(
    value_ref,
    taps_ref,
    step_ref,
    decay_ref,
    skip_ref,
    in_basis_ref,
    out_basis_ref,
    out_grad_ref,
    conv_ref,
    in_out_ref,
    out_out_ref,
    mixed,
    weighted,
    grad_weighted,
    slope,
    base,
    in_part,
    out_part,
    value_grad,
    entering,
    leaving,
    running,
    edge,
    sum_rows,
    sum_columns,
    step_columns,
    scale_columns,
    grow_columns,
    block_row,
    prefix_row,
    suffix_row,
    tiles,
    landed,
    outs,
    returned,
    decay_tiles,
    decay_landed,
    halo,
    send_sem,
    recv_sem,
):
    me = lax.axis_index("seq")
    devices = lax.axis_size("seq")
    heads = step_ref.shape[0]
    blocks = step_ref.shape[1] // SPAN
    width = heads * P_SIZE
    length = blocks * SPAN
    strips = width // LANES
    depth = tiles.shape[2]

    barrier = pltpu.get_barrier_semaphore()

    def greet(step, carry):
        pl.semaphore_signal(
            barrier, inc=1, device_id={"seq": (me + step) % devices}, device_id_type=MESH
        )
        return carry

    lax.fori_loop(1, devices, greet, 0)

    lane = lax.broadcasted_iota(jnp.int32, (heads, SPAN), 1)
    ends = []
    for block in range(blocks):
        part = slice(block * SPAN, (block + 1) * SPAN)
        total = decay_ref[:, part]
        shift = 1
        while shift < SPAN:
            total = total + jnp.where(lane >= shift, pltpu.roll(total, shift, 1), 0.0)
            shift *= 2
        last = total[:, SPAN - 1 : SPAN]
        steps = step_ref[:, part]
        sum_rows[block] = total
        sum_columns[block] = total.T
        step_columns[block] = steps.T
        scale_columns[block] = (jnp.exp(last - total) * steps).T
        grow_columns[block] = jnp.exp(total).T
        block_row[block] = head_row(jnp.exp(last), width)
        ends.append(last)
    before = jnp.zeros((heads, 1), F32)
    after = jnp.zeros((heads, 1), F32)
    for block in range(blocks):
        prefix_row[block] = head_row(jnp.exp(before), width)
        before = before + ends[block]
        back = blocks - 1 - block
        suffix_row[back] = head_row(jnp.exp(after), width)
        after = after + ends[back]
    device_row = head_row(jnp.exp(before), width)
    for strip in range(strips):
        decay_tiles[strip] = device_row[:, strip * LANES : (strip + 1) * LANES]

    def rows_of(block):
        return pl.ds(pl.multiple_of(block * SPAN, SPAN), SPAN)

    def remote(place, source, target_ref, target):
        return pltpu.make_async_remote_copy(
            src_ref=source,
            dst_ref=target_ref,
            send_sem=send_sem.at[place],
            recv_sem=recv_sem.at[place],
            device_id={"seq": target},
            device_id_type=MESH,
        )

    def wait_all(place, sent, got):
        remote(place, sent, sent, (me + 1) % devices).wait_send()
        remote(place, got, got, (me + 1) % devices).wait_recv()

    rest = pl.ds(1, devices - 1)

    def scatter_state(way):
        for row in range(N // depth):
            for strip in range(strips):
                tiles[way, row * strips + strip] = running[
                    row * depth : (row + 1) * depth, strip * LANES : (strip + 1) * LANES
                ].astype(BF16)

        def one(step, carry):
            target = (me + step) % devices
            remote(way, tiles.at[way, target], landed.at[way, step], target).start()
            return carry

        lax.fori_loop(1, devices, one, 0)
        landed[way, 0] = tiles[way, me]

    def scan_state(way):
        wait_all(way, tiles.at[way, rest], landed.at[way, rest])
        state = jnp.zeros((depth, LANES), F32)

        def one(turn, state):
            place = turn if way == 0 else devices - 1 - turn
            slot = (me - place + devices) % devices
            outs[way, place] = state.astype(BF16)
            return decay_landed[slot][0:1] * state + landed[way, slot].astype(F32)

        lax.fori_loop(0, devices, one, state)

        def back(step, carry):
            target = (me + step) % devices
            remote(3 + way, outs.at[way, target], returned.at[way, me], target).start()
            return carry

        lax.fori_loop(1, devices, back, 0)
        returned[way, me] = outs[way, me]

    def collect_state(way):
        wait_all(3 + way, outs.at[way, rest], returned.at[way, rest])
        for row in range(N // depth):
            for strip in range(strips):
                edge[
                    way, row * depth : (row + 1) * depth, strip * LANES : (strip + 1) * LANES
                ] = returned[way, row * strips + strip].astype(F32)

    running[...] = jnp.zeros_like(running)

    def ahead(block, carry):
        rows = rows_of(block)
        value = value_ref[rows].astype(F32)
        sigmoid = jax.nn.sigmoid(value)
        act = (value * sigmoid).astype(BF16)
        mixed[rows] = act
        slope[rows] = sigmoid + value * sigmoid * (1.0 - sigmoid)
        scaled = (act.astype(F32) * widen(scale_columns[block])).astype(BF16)
        weighted[rows] = scaled
        entering[block] = running[...]
        running[...] = block_row[block][0:1] * running[...] + dot(in_basis_ref[rows], scaled, 0, 0)
        return carry

    lax.fori_loop(0, blocks, ahead, 0)

    pl.semaphore_wait(barrier, devices - 1)

    def send_decay(step, carry):
        target = (me + step) % devices
        remote(2, decay_tiles.at[target % strips], decay_landed.at[step], target).start()
        return carry

    lax.fori_loop(1, devices, send_decay, 0)
    decay_landed[0] = decay_tiles[me % strips]
    scatter_state(0)

    running[...] = jnp.zeros_like(running)

    def behind(turn, carry):
        block = blocks - 1 - turn
        rows = rows_of(block)
        scaled = (out_grad_ref[rows].astype(F32) * widen(grow_columns[block])).astype(BF16)
        grad_weighted[rows] = scaled
        leaving[block] = running[...]
        running[...] = block_row[block][0:1] * running[...] + dot(
            out_basis_ref[rows], scaled, 0, 0
        )
        return carry

    lax.fori_loop(0, blocks, behind, 0)
    scatter_state(1)
    wait_all(2, decay_landed.at[rest], decay_landed.at[rest])
    scan_state(0)

    lane_row = lax.broadcasted_iota(jnp.int32, (1, LANES), 1)
    left_half = jnp.where(lane_row < P_SIZE, 1.0, 0.0).astype(BF16)
    right_half = jnp.where(lane_row < P_SIZE, 0.0, 1.0).astype(BF16)

    def inside(block, carry):
        rows = rows_of(block)
        in_basis, out_basis = in_basis_ref[rows], out_basis_ref[rows]
        source = lax.broadcasted_iota(jnp.int32, (SPAN, SPAN), 0)
        reader = lax.broadcasted_iota(jnp.int32, (SPAN, SPAN), 1)
        lower = reader >= source
        scores = dot(in_basis, out_basis, 1, 1)
        total = jnp.zeros((SPAN, SPAN), F32)
        for strip in range(strips):
            span = slice(strip * LANES, (strip + 1) * LANES)
            grad_pair = out_grad_ref[rows, span]
            act_pair = mixed[rows, span]
            act_two = jnp.concatenate([act_pair * left_half, act_pair * right_half], axis=0)
            grad_two = jnp.concatenate([grad_pair * left_half, grad_pair * right_half], axis=0)
            grad_mixed = dot(act_two, grad_pair, 1, 1)
            weights = []
            for side in range(2):
                head = 2 * strip + side
                gap = sum_rows[block, head : head + 1, :] - sum_columns[block][:, head : head + 1]
                mask = (
                    jnp.exp(jnp.where(lower, gap, -1e30)) * step_columns[block][:, head : head + 1]
                )
                weights.append((mask * scores).astype(BF16))
                total = total + mask * grad_mixed[side * SPAN : (side + 1) * SPAN]
            inner = dot(jnp.concatenate(weights, axis=1), grad_two, 1, 0)
            base[rows, span] = inner + skip_ref[:, span] * grad_pair.astype(F32)
        in_part[rows] = dot(total.astype(BF16), out_basis, 1, 0)
        out_part[rows] = dot(total.T.astype(BF16), in_basis, 1, 0)
        return carry

    split = blocks // 2
    lax.fori_loop(0, split, inside, 0)
    scan_state(1)
    lax.fori_loop(split, blocks, inside, 0)
    collect_state(0)
    collect_state(1)

    def close(block, carry):
        rows = rows_of(block)
        enter = (entering[block] + prefix_row[block][0:1] * edge[0]).astype(BF16)
        leave = (leaving[block] + suffix_row[block][0:1] * edge[1]).astype(BF16)
        carried = dot(in_basis_ref[rows], leave, 1, 0)
        value_grad[rows] = (base[rows] + widen(scale_columns[block]) * carried) * slope[rows]
        in_out_ref[rows] = (in_part[rows] + dot(weighted[rows], leave, 1, 1)).astype(BF16)
        out_out_ref[rows] = (out_part[rows] + dot(grad_weighted[rows], enter, 1, 1)).astype(BF16)
        return carry

    close(0, 0)
    ahead_rows = remote(5, value_grad.at[pl.ds(0, 8)], halo, (me + devices - 1) % devices)
    ahead_rows.start()
    lax.fori_loop(1, blocks, close, 0)
    ahead_rows.wait()
    value_grad[pl.ds(length, 8)] = jnp.where(me == devices - 1, 0.0, halo[...])

    def filtered(block, carry):
        start = pl.multiple_of(block * SPAN, SPAN)
        window = value_grad[pl.ds(start, SPAN + 8)]
        summed = taps_ref[0:1] * window[0:SPAN]
        for tap in range(1, KW):
            summed = summed + taps_ref[tap : tap + 1] * window[tap : tap + SPAN]
        conv_ref[pl.ds(start, SPAN)] = summed.astype(BF16)
        return carry

    lax.fori_loop(0, blocks, filtered, 0)


def mixer_part(value, taps, step, decay, skip, in_basis, out_basis, out_grad):
    devices = lax.axis_size("seq")
    heads, length = step.shape
    blocks = length // SPAN
    width = heads * P_SIZE
    strips = width // LANES
    depth = N * strips // devices
    skip_row = jnp.repeat(skip, P_SIZE)[None]
    vmem = pl.BlockSpec(memory_space=pltpu.VMEM)
    return pl.pallas_call(
        mixer_kernel,
        out_shape=(
            jax.ShapeDtypeStruct((length, width), BF16),
            jax.ShapeDtypeStruct((length, N), BF16),
            jax.ShapeDtypeStruct((length, N), BF16),
        ),
        in_specs=[vmem] * 8,
        out_specs=(vmem,) * 3,
        scratch_shapes=[
            pltpu.VMEM((length, width), BF16),
            pltpu.VMEM((length, width), BF16),
            pltpu.VMEM((length, width), BF16),
            pltpu.VMEM((length, width), F32),
            pltpu.VMEM((length, width), F32),
            pltpu.VMEM((length, N), F32),
            pltpu.VMEM((length, N), F32),
            pltpu.VMEM((length + 8, width), F32),
            pltpu.VMEM((blocks, N, width), F32),
            pltpu.VMEM((blocks, N, width), F32),
            pltpu.VMEM((N, width), F32),
            pltpu.VMEM((2, N, width), F32),
            pltpu.VMEM((blocks, heads, SPAN), F32),
            pltpu.VMEM((blocks, SPAN, heads), F32),
            pltpu.VMEM((blocks, SPAN, heads), F32),
            pltpu.VMEM((blocks, SPAN, heads), F32),
            pltpu.VMEM((blocks, SPAN, heads), F32),
            pltpu.VMEM((blocks, 8, width), F32),
            pltpu.VMEM((blocks, 8, width), F32),
            pltpu.VMEM((blocks, 8, width), F32),
            pltpu.VMEM((2, devices, depth, LANES), BF16),
            pltpu.VMEM((2, devices, depth, LANES), BF16),
            pltpu.VMEM((2, devices, depth, LANES), BF16),
            pltpu.VMEM((2, devices, depth, LANES), BF16),
            pltpu.VMEM((strips, 8, LANES), F32),
            pltpu.VMEM((devices, 8, LANES), F32),
            pltpu.VMEM((8, width), F32),
            pltpu.SemaphoreType.DMA((6,)),
            pltpu.SemaphoreType.DMA((6,)),
        ],
        compiler_params=pltpu.CompilerParams(
            collective_id=2, has_side_effects=True, vmem_limit_bytes=60 * 1024 * 1024
        ),
        name="mixer_part",
    )(value, taps, step, decay, skip_row, in_basis, out_basis, out_grad)


def shards(
    grad_out,
    expert_input,
    expert_index,
    route_weight,
    up_weight,
    down_weight,
    out_weight,
    conv_value,
    conv_weight,
    step_size,
    log_decay,
    skip_gain,
    input_basis,
    output_basis,
):
    residual_grad, out_grad = expert_part(
        grad_out,
        expert_input,
        expert_index,
        route_weight,
        up_weight[0],
        down_weight[0],
        out_weight,
    )
    conv_grad, in_grad, out_part = mixer_part(
        conv_value,
        conv_weight,
        step_size,
        log_decay,
        skip_gain,
        input_basis,
        output_basis,
        out_grad,
    )
    return (residual_grad, conv_grad, in_grad, out_part)


def solution(mesh):
    in_specs = (
        P(("seq", "expert"), None),
        P(("seq", "expert"), None),
        P(("seq", "expert"), None),
        P(("seq", "expert"), None),
        P("expert", None, None),
        P("expert", None, None),
        P("expert", None),
        P("seq", "expert"),
        P(None, "expert"),
        P("expert", "seq"),
        P("expert", "seq"),
        P("expert"),
        P("seq", "expert"),
        P("seq", "expert"),
    )
    out_specs = (
        P(("seq", "expert"), None),
        P("seq", "expert"),
        P("seq", "expert"),
        P("seq", "expert"),
    )
    return jax.shard_map(shards, mesh=mesh, in_specs=in_specs, out_specs=out_specs, check_vma=False)
```

```python
import functools

import jax
import jax.numpy as jnp
from jax import lax
from jax.experimental import pallas as pl
from jax.experimental.pallas import tpu as pltpu
from jax.sharding import PartitionSpec as P

P_SIZE = 64
N = 128
KW = 4
SPAN = 128
LANES = 128
MESH = pl.DeviceIdType.MESH
F32 = jnp.float32
BF16 = jnp.bfloat16


def dot(a, b, left, right):
    return lax.dot_general(a, b, (((left,), (right,)), ((), ())), preferred_element_type=F32)


def widen(columns):
    lane = lax.broadcasted_iota(jnp.int32, (columns.shape[0], LANES), 1)
    parts = []
    for pair in range(columns.shape[1] // 2):
        one, two = columns[:, 2 * pair : 2 * pair + 1], columns[:, 2 * pair + 1 : 2 * pair + 2]
        parts.append(jnp.where(lane < P_SIZE, one, two))
    return jnp.concatenate(parts, axis=1)


def head_row(column, width):
    heads = column.shape[0]
    lane = lax.broadcasted_iota(jnp.int32, (heads, width), 1)
    head = lax.broadcasted_iota(jnp.int32, (heads, width), 0)
    chosen = jnp.where(lane // P_SIZE == head, column, 0.0)
    return jnp.broadcast_to(jnp.sum(chosen, axis=0, keepdims=True), (8, width))


def layer_kernel(
    input_ref,
    grad_ref,
    route_ref,
    up_ref,
    down_ref,
    out_weight_ref,
    value_hbm,
    in_basis_hbm,
    out_basis_hbm,
    taps_ref,
    step_ref,
    decay_ref,
    skip_ref,
    residual_ref,
    conv_ref,
    in_out_ref,
    out_out_ref,
    inputs,
    grads,
    partial,
    gathered,
    sibling_part,
    far_part,
    near_part,
    summed,
    routes,
    hidden,
    up,
    down,
    out_weight,
    out_grad,
    value_ref,
    in_basis_ref,
    out_basis_ref,
    mixed,
    weighted,
    grad_weighted,
    slope,
    masks,
    weights,
    in_part,
    out_part,
    value_grad,
    entering,
    leaving,
    running,
    edge,
    sum_rows,
    sum_columns,
    step_columns,
    scale_columns,
    grow_columns,
    block_row,
    prefix_row,
    suffix_row,
    tiles,
    landed,
    outs,
    returned,
    decay_tiles,
    decay_landed,
    halo,
    local_sem,
    send_sem,
    recv_sem,
    seq_send,
    seq_recv,
):
    here = lax.axis_index("seq")
    devices = lax.axis_size("seq")
    heads = step_ref.shape[0]
    blocks = step_ref.shape[1] // SPAN
    width = heads * P_SIZE
    length = blocks * SPAN
    strips = width // LANES
    depth = tiles.shape[2]

    me = lax.axis_index("expert")
    count = lax.axis_size("expert")
    chips = count // 2
    chip, core = me // 2, me % 2
    rows = input_ref.shape[0]
    half = rows // 2
    low, high, whole = pl.ds(0, half), pl.ds(half, half), pl.ds(0, rows)
    other, other_low, other_high = pl.ds(rows, rows), pl.ds(rows, half), pl.ds(rows + half, half)

    def device(chip_step, core_step):
        return ((chip + chip_step) % chips) * 2 + (core + core_step) % 2

    sibling, right, left = device(0, 1), device(1, 0), device(chips - 1, 0)
    copies = {}

    def send(name, source, target_ref, target):
        place = len(copies)
        copies[name] = pltpu.make_async_remote_copy(
            src_ref=source,
            dst_ref=target_ref,
            send_sem=send_sem.at[place],
            recv_sem=recv_sem.at[place],
            device_id={"expert": target},
            device_id_type=MESH,
        )
        copies[name].start()

    def arrived(*names):
        for name in names:
            copies[name].wait_recv()

    loads = []
    for place, (source, target) in enumerate(
        (
            (input_ref, inputs.at[0, whole]),
            (up_ref, up),
            (route_ref.at[me], routes.at[0]),
            (grad_ref, grads.at[0, whole]),
            (down_ref, down),
            (out_weight_ref, out_weight),
            (value_hbm, value_ref),
            (in_basis_hbm, in_basis_ref),
            (out_basis_hbm, out_basis_ref),
        )
    ):
        loads.append(pltpu.make_async_copy(source, target, local_sem.at[place]))
        loads[-1].start()

    barrier = pltpu.get_barrier_semaphore()
    for step in range(1, count):
        pl.semaphore_signal(
            barrier, inc=1, device_id={"expert": (me + step) % count}, device_id_type=MESH
        )

    def greet(step, carry):
        pl.semaphore_signal(
            barrier, inc=1, device_id={"seq": (here + step) % devices}, device_id_type=MESH
        )
        return carry

    lax.fori_loop(1, devices, greet, 0)
    pl.semaphore_wait(barrier, count + devices - 2)

    def first(tag, source, buffer):
        send(tag + "r1", source.at[low], buffer.at[1, low], right)
        send(tag + "l1", source.at[high], buffer.at[2, high], left)
        send(tag + "s0", source, buffer.at[0, other], sibling)

    def second(tag, source, buffer):
        send(tag + "r2", source.at[high], buffer.at[1, high], right)
        send(tag + "l2", source.at[low], buffer.at[2, low], left)

    def forward(tag, buffer):
        arrived(tag + "r1")
        send(tag + "r3", buffer.at[1, low], buffer.at[3, low], right)
        send(tag + "s1", buffer.at[1, low], buffer.at[1, other_low], sibling)
        arrived(tag + "l1")
        send(tag + "l3", buffer.at[2, high], buffer.at[3, high], left)
        send(tag + "s2", buffer.at[2, high], buffer.at[2, other_high], sibling)

    def share_near(tag, buffer):
        arrived(tag + "r2")
        send(tag + "s3", buffer.at[1, high], buffer.at[1, other_high], sibling)
        arrived(tag + "l2")
        send(tag + "s4", buffer.at[2, low], buffer.at[2, other_low], sibling)

    def share_far(tag, buffer):
        arrived(tag + "r3")
        send(tag + "s5", buffer.at[3, low], buffer.at[3, other_low], sibling)
        arrived(tag + "l3")
        send(tag + "s6", buffer.at[3, high], buffer.at[3, other_high], sibling)

    first("x", input_ref, inputs)
    first("g", grad_ref, grads)
    for chip_step, slot in ((0, 0), (1, 1), (chips - 1, 2), (2, 3)):
        for core_step in range(2):
            if (chip_step, core_step) != (0, 0):
                target = device(chip_step, core_step)
                send(
                    "w%d%d" % (slot, core_step),
                    route_ref.at[target],
                    routes.at[2 * slot + core_step],
                    target,
                )
    second("x", input_ref, inputs)

    lane = lax.broadcasted_iota(jnp.int32, (heads, SPAN), 1)
    ends = []
    for block in range(blocks):
        part = slice(block * SPAN, (block + 1) * SPAN)
        total = decay_ref[:, part]
        shift = 1
        while shift < SPAN:
            total = total + jnp.where(lane >= shift, pltpu.roll(total, shift, 1), 0.0)
            shift *= 2
        last = total[:, SPAN - 1 : SPAN]
        steps = step_ref[:, part]
        sum_rows[block] = total
        sum_columns[block] = total.T
        step_columns[block] = steps.T
        scale_columns[block] = (jnp.exp(last - total) * steps).T
        grow_columns[block] = jnp.exp(total).T
        block_row[block] = head_row(jnp.exp(last), width)
        ends.append(last)
    before = jnp.zeros((heads, 1), F32)
    after = jnp.zeros((heads, 1), F32)
    for block in range(blocks):
        prefix_row[block] = head_row(jnp.exp(before), width)
        before = before + ends[block]
        back = blocks - 1 - block
        suffix_row[back] = head_row(jnp.exp(after), width)
        after = after + ends[back]
    device_row = head_row(jnp.exp(before), width)
    for strip in range(strips):
        decay_tiles[strip] = device_row[:, strip * LANES : (strip + 1) * LANES]

    def rows_of(block):
        return pl.ds(pl.multiple_of(block * SPAN, SPAN), SPAN)

    def remote(place, source, target_ref, target):
        return pltpu.make_async_remote_copy(
            src_ref=source,
            dst_ref=target_ref,
            send_sem=seq_send.at[place],
            recv_sem=seq_recv.at[place],
            device_id={"seq": target},
            device_id_type=MESH,
        )

    def wait_all(place, sent, got):
        remote(place, sent, sent, (here + 1) % devices).wait_send()
        remote(place, got, got, (here + 1) % devices).wait_recv()

    rest = pl.ds(1, devices - 1)

    def scatter_state(way):
        for row in range(N // depth):
            for strip in range(strips):
                tiles[way, row * strips + strip] = running[
                    row * depth : (row + 1) * depth, strip * LANES : (strip + 1) * LANES
                ].astype(BF16)

        def one(step, carry):
            target = (here + step) % devices
            remote(way, tiles.at[way, target], landed.at[way, step], target).start()
            return carry

        lax.fori_loop(1, devices, one, 0)
        landed[way, 0] = tiles[way, here]

    def scan_state(way):
        wait_all(way, tiles.at[way, rest], landed.at[way, rest])
        state = jnp.zeros((depth, LANES), F32)

        def one(turn, state):
            place = turn if way == 0 else devices - 1 - turn
            slot = (here - place + devices) % devices
            outs[way, place] = state.astype(BF16)
            return decay_landed[slot][0:1] * state + landed[way, slot].astype(F32)

        lax.fori_loop(0, devices, one, state)

        def back(step, carry):
            target = (here + step) % devices
            remote(3 + way, outs.at[way, target], returned.at[way, here], target).start()
            return carry

        lax.fori_loop(1, devices, back, 0)
        returned[way, here] = outs[way, here]

    def collect_state(way):
        wait_all(3 + way, outs.at[way, rest], returned.at[way, rest])
        for row in range(N // depth):
            for strip in range(strips):
                edge[
                    way, row * depth : (row + 1) * depth, strip * LANES : (strip + 1) * LANES
                ] = returned[way, row * strips + strip].astype(F32)


    lane_row = lax.broadcasted_iota(jnp.int32, (1, LANES), 1)
    left_half = jnp.where(lane_row < P_SIZE, 1.0, 0.0).astype(BF16)
    right_half = jnp.where(lane_row < P_SIZE, 0.0, 1.0).astype(BF16)

    def weigh(block, carry):
        rows = rows_of(block)
        source = lax.broadcasted_iota(jnp.int32, (SPAN, SPAN), 0)
        reader = lax.broadcasted_iota(jnp.int32, (SPAN, SPAN), 1)
        lower = reader >= source
        scores = dot(in_basis_ref[rows], out_basis_ref[rows], 1, 1)
        for head in range(heads):
            gap = sum_rows[block, head : head + 1, :] - sum_columns[block][:, head : head + 1]
            mask = jnp.exp(jnp.where(lower, gap, -1e30)) * step_columns[block][:, head : head + 1]
            masks[block, head] = mask
            weights[block, :, head * SPAN : (head + 1) * SPAN] = (mask * scores).astype(BF16)
        return carry

    def local_start(block):
        rows = rows_of(block)
        scaled = (out_grad[rows].astype(F32) * widen(grow_columns[block])).astype(BF16)
        grad_weighted[rows] = scaled
        leaving[block] = dot(out_basis_ref[rows], scaled, 0, 0)

    def inside(block):
        rows = rows_of(block)
        in_basis, out_basis = in_basis_ref[rows], out_basis_ref[rows]
        total = jnp.zeros((SPAN, SPAN), F32)
        skip_row = widen(skip_ref[...])
        for strip in range(strips):
            span = slice(strip * LANES, (strip + 1) * LANES)
            grad_pair = out_grad[rows, span]
            act_pair = mixed[rows, span]
            act_two = jnp.concatenate([act_pair * left_half, act_pair * right_half], axis=0)
            grad_two = jnp.concatenate([grad_pair * left_half, grad_pair * right_half], axis=0)
            grad_mixed = dot(act_two, grad_pair, 1, 1)
            for side in range(2):
                total = total + masks[block, 2 * strip + side] * (
                    grad_mixed[side * SPAN : (side + 1) * SPAN]
                )
            pair = weights[block, :, 2 * strip * SPAN : 2 * (strip + 1) * SPAN]
            value_grad[rows, span] = dot(pair, grad_two, 1, 0) + skip_row[
                :, span
            ] * grad_pair.astype(F32)
        in_part[rows] = dot(total.astype(BF16), out_basis, 1, 0)
        out_part[rows] = dot(total.T.astype(BF16), in_basis, 1, 0)

    def chain_back():
        running[...] = jnp.zeros_like(running)

        def behind(turn, carry):
            block = blocks - 1 - turn
            added = leaving[block]
            leaving[block] = running[...]
            running[...] = block_row[block][0:1] * running[...] + added
            return carry

        lax.fori_loop(0, blocks, behind, 0)

    def close_out(block, carry):
        rows = rows_of(block)
        enter = (entering[block] + prefix_row[block][0:1] * edge[0]).astype(BF16)
        out_out_ref[rows] = (out_part[rows] + dot(grad_weighted[rows], enter, 1, 1)).astype(BF16)
        return carry

    def close(block, carry):
        rows = rows_of(block)
        leave = (leaving[block] + suffix_row[block][0:1] * edge[1]).astype(BF16)
        carried = dot(in_basis_ref[rows], leave, 1, 0)
        value_grad[rows] = (value_grad[rows] + widen(scale_columns[block]) * carried) * slope[rows]
        in_out_ref[rows] = (in_part[rows] + dot(weighted[rows], leave, 1, 1)).astype(BF16)
        return carry

    def inner_blocks(chip_step, work):
        def one(core_step, carry):
            work(device(chip_step, core_step))
            return carry

        lax.fori_loop(0, 2, one, 0)

    def both(block):
        local_start(block)
        inside(block)

    def before(slot):
        hidden[slot] = 2.0 * jnp.maximum(dot(inputs[slot], up[...], 1, 0), 0.0)

    def after(slot):
        column = jnp.concatenate(
            [routes[2 * slot].T[:, 0:1], routes[2 * slot + 1].T[:, 0:1]], axis=0
        )
        back = dot(grads[slot], down[...], 1, 1) * column
        inner = (hidden[slot] * back).astype(BF16)
        partial[slot] = dot(inner, up[...], 1, 1).astype(BF16)
        send("p%d" % slot, partial.at[slot, other], sibling_part.at[slot], sibling)

    loads[0].wait()
    loads[1].wait()
    arrived("xs0")
    before(0)
    forward("x", inputs)
    for place in (6, 7, 8):
        loads[place].wait()
    running[...] = jnp.zeros_like(running)

    def ahead(block, carry):
        rows = rows_of(block)
        value = value_ref[rows].astype(F32)
        sigmoid = jax.nn.sigmoid(value)
        act = (value * sigmoid).astype(BF16)
        mixed[rows] = act
        slope[rows] = sigmoid + value * sigmoid * (1.0 - sigmoid)
        scaled = (act.astype(F32) * widen(scale_columns[block])).astype(BF16)
        weighted[rows] = scaled
        entering[block] = running[...]
        running[...] = block_row[block][0:1] * running[...] + dot(in_basis_ref[rows], scaled, 0, 0)
        return carry

    lax.fori_loop(0, blocks, ahead, 0)

    def send_decay(step, carry):
        target = (here + step) % devices
        remote(2, decay_tiles.at[target % strips], decay_landed.at[step], target).start()
        return carry

    lax.fori_loop(1, devices, send_decay, 0)
    decay_landed[0] = decay_tiles[here % strips]
    scatter_state(0)

    loads[2].wait()
    for slot, core_step in ((0, 1), (1, 0), (1, 1), (2, 0), (2, 1), (3, 0), (3, 1)):
        arrived("w%d%d" % (slot, core_step))
    loads[3].wait()
    loads[4].wait()
    forward("g", grads)
    second("g", grad_ref, grads)
    arrived("gs0")
    after(0)
    lax.fori_loop(0, blocks, weigh, 0)
    share_near("x", inputs)
    arrived("xs1", "xs3")
    before(1)
    arrived("xs2", "xs4")
    before(2)
    share_far("x", inputs)
    arrived("xs5", "xs6")
    before(3)
    wait_all(2, decay_landed.at[rest], decay_landed.at[rest])
    scan_state(0)
    share_far("g", grads)
    arrived("gs5", "gs6")
    after(3)
    share_near("g", grads)
    arrived("p3")
    summed[0] = partial[3, whole] + sibling_part[3]
    send("fr", summed.at[0, low], far_part.at[0], right)
    send("fl", summed.at[0, high], far_part.at[1], left)
    arrived("gs2", "gs4")
    after(2)
    arrived("gs1", "gs3")
    after(1)
    arrived("p2")
    summed[1, high] = partial[2, high] + sibling_part[2, high]
    send("nr1", summed.at[1, high], near_part.at[0, high], right)
    arrived("p1")
    summed[2, low] = partial[1, low] + sibling_part[1, low]
    send("nl1", summed.at[2, low], near_part.at[1, low], left)

    def three(a, b, c):
        return (a.astype(F32) + b.astype(F32) + c.astype(F32)).astype(BF16)

    arrived("fr")
    summed[1, low] = three(partial[2, low], sibling_part[2, low], far_part[0])
    send("nr2", summed.at[1, low], near_part.at[0, low], right)
    arrived("fl")
    summed[2, high] = three(partial[1, high], sibling_part[1, high], far_part[1])
    send("nl2", summed.at[2, high], near_part.at[1, high], left)
    loads[5].wait()
    arrived("p0")

    def finish(part):
        gathered[0, part] = (
            grads[0, part].astype(F32)
            + partial[0, part].astype(F32)
            + sibling_part[0, part].astype(F32)
            + near_part[0, part].astype(F32)
            + near_part[1, part].astype(F32)
        ).astype(BF16)

    arrived("nr1", "nl1", "nr2", "nl2")
    finish(low)
    finish(high)
    own = gathered.at[0, whole]
    first("o", own, gathered)
    second("o", own, gathered)
    store = pltpu.make_async_copy(own, residual_ref, local_sem.at[0])
    store.start()

    def project(slot, chip_step):
        product = dot(gathered[slot], out_weight[...], 1, 1).astype(BF16)
        for core_step in range(2):
            start = pl.multiple_of(device(chip_step, core_step) * rows, rows)
            out_grad[pl.ds(start, rows)] = product[core_step * rows : (core_step + 1) * rows]

    arrived("os0")
    project(0, 0)
    inner_blocks(0, both)
    forward("o", gathered)
    share_near("o", gathered)
    arrived("os1", "os3")
    project(1, chips - 1)
    inner_blocks(chips - 1, both)
    arrived("os2", "os4")
    project(2, 1)
    inner_blocks(1, both)
    share_far("o", gathered)
    arrived("os5", "os6")
    project(3, 2)
    inner_blocks(2, local_start)
    chain_back()
    scatter_state(1)
    inner_blocks(2, inside)
    scan_state(1)
    collect_state(0)
    lax.fori_loop(0, blocks, close_out, 0)
    collect_state(1)
    close(0, 0)
    ahead_rows = remote(5, value_grad.at[pl.ds(0, 8)], halo, (here + devices - 1) % devices)
    ahead_rows.start()
    lax.fori_loop(1, blocks, close, 0)
    ahead_rows.wait()
    value_grad[pl.ds(length, 8)] = jnp.where(here == devices - 1, 0.0, halo[...])

    def filtered(block, carry):
        start = pl.multiple_of(block * SPAN, SPAN)
        window = value_grad[pl.ds(start, SPAN + 8)]
        summed = taps_ref[0:1] * window[0:SPAN]
        for tap in range(1, KW):
            summed = summed + taps_ref[tap : tap + 1] * window[tap : tap + SPAN]
        conv_ref[pl.ds(start, SPAN)] = summed.astype(BF16)
        return carry

    lax.fori_loop(0, blocks, filtered, 0)


    store.wait()
    for copy in copies.values():
        copy.wait_send()


def layer_part(
    grad_out,
    expert_input,
    expert_index,
    route_weight,
    up,
    down,
    out_weight,
    value,
    taps,
    step,
    decay,
    skip,
    in_basis,
    out_basis,
):
    count = lax.axis_size("expert")
    rows, wide = grad_out.shape
    inner = up.shape[1]
    match = expert_index[None] == jnp.arange(count, dtype=jnp.int32)[:, None, None]
    table = jnp.sum(jnp.where(match, route_weight[None], 0.0), axis=2)
    routes = jnp.broadcast_to(table[:, None, :], (count, 8, rows))
    copies = 64
    devices = lax.axis_size("seq")
    heads, length = step.shape
    blocks = length // SPAN
    width = heads * P_SIZE
    strips = width // LANES
    depth = N * strips // devices
    hbm = pl.BlockSpec(memory_space=pl.ANY)
    vmem = pl.BlockSpec(memory_space=pltpu.VMEM)
    return pl.pallas_call(
        layer_kernel,
        out_shape=(
            jax.ShapeDtypeStruct((rows, wide), BF16),
            jax.ShapeDtypeStruct((length, width), BF16),
            jax.ShapeDtypeStruct((length, N), BF16),
            jax.ShapeDtypeStruct((length, N), BF16),
        ),
        in_specs=[hbm] * 9 + [vmem] * 4,
        out_specs=(hbm, vmem, vmem, vmem),
        scratch_shapes=[
            pltpu.VMEM((4, 2 * rows, wide), BF16),
            pltpu.VMEM((4, 2 * rows, wide), BF16),
            pltpu.VMEM((4, 2 * rows, wide), BF16),
            pltpu.VMEM((4, 2 * rows, wide), BF16),
            pltpu.VMEM((4, rows, wide), BF16),
            pltpu.VMEM((2, rows // 2, wide), BF16),
            pltpu.VMEM((2, rows, wide), BF16),
            pltpu.VMEM((3, rows, wide), BF16),
            pltpu.VMEM((8, 8, rows), F32),
            pltpu.VMEM((4, 2 * rows, inner), F32),
            pltpu.VMEM((wide, inner), BF16),
            pltpu.VMEM((inner, wide), BF16),
            pltpu.VMEM((width, wide), BF16),
            pltpu.VMEM((length, width), BF16),
            pltpu.VMEM((length, width), BF16),
            pltpu.VMEM((length, N), BF16),
            pltpu.VMEM((length, N), BF16),
            pltpu.VMEM((length, width), BF16),
            pltpu.VMEM((length, width), BF16),
            pltpu.VMEM((length, width), BF16),
            pltpu.VMEM((length, width), F32),
            pltpu.VMEM((blocks, heads, SPAN, SPAN), F32),
            pltpu.VMEM((blocks, SPAN, heads * SPAN), BF16),
            pltpu.VMEM((length, N), F32),
            pltpu.VMEM((length, N), F32),
            pltpu.VMEM((length + 8, width), F32),
            pltpu.VMEM((blocks, N, width), F32),
            pltpu.VMEM((blocks, N, width), F32),
            pltpu.VMEM((N, width), F32),
            pltpu.VMEM((2, N, width), F32),
            pltpu.VMEM((blocks, heads, SPAN), F32),
            pltpu.VMEM((blocks, SPAN, heads), F32),
            pltpu.VMEM((blocks, SPAN, heads), F32),
            pltpu.VMEM((blocks, SPAN, heads), F32),
            pltpu.VMEM((blocks, SPAN, heads), F32),
            pltpu.VMEM((blocks, 8, width), F32),
            pltpu.VMEM((blocks, 8, width), F32),
            pltpu.VMEM((blocks, 8, width), F32),
            pltpu.VMEM((2, devices, depth, LANES), BF16),
            pltpu.VMEM((2, devices, depth, LANES), BF16),
            pltpu.VMEM((2, devices, depth, LANES), BF16),
            pltpu.VMEM((2, devices, depth, LANES), BF16),
            pltpu.VMEM((strips, 8, LANES), F32),
            pltpu.VMEM((devices, 8, LANES), F32),
            pltpu.VMEM((8, width), F32),
            pltpu.SemaphoreType.DMA((9,)),
            pltpu.SemaphoreType.DMA((copies,)),
            pltpu.SemaphoreType.DMA((copies,)),
            pltpu.SemaphoreType.DMA((6,)),
            pltpu.SemaphoreType.DMA((6,)),
        ],
        compiler_params=pltpu.CompilerParams(
            collective_id=1, has_side_effects=True, vmem_limit_bytes=67043328
        ),
        name="layer_part",
    )(
        expert_input,
        grad_out,
        routes,
        up,
        down,
        out_weight,
        value,
        in_basis,
        out_basis,
        taps,
        step,
        decay,
        skip[None],
    )


def results_kernel(*refs):
    sources, targets, held, (in_sem, out_sem) = refs[0:4], refs[4:8], refs[8:12], refs[12:14]
    loads, stores = [], []
    for place in range(4):
        loads.append(pltpu.make_async_copy(sources[place], held[place], in_sem.at[place]))
        loads[-1].start()
    for place in range(4):
        loads[place].wait()
        stores.append(pltpu.make_async_copy(held[place], targets[place], out_sem.at[place]))
        stores[-1].start()
    for store in stores:
        store.wait()


def results(*arrays):
    shapes = [jax.ShapeDtypeStruct(array.shape, array.dtype) for array in arrays]
    hbm = pl.BlockSpec(memory_space=pl.ANY)
    return pl.pallas_call(
        results_kernel,
        out_shape=tuple(shapes),
        in_specs=[hbm] * len(arrays),
        out_specs=(hbm,) * len(arrays),
        scratch_shapes=[pltpu.VMEM(array.shape, array.dtype) for array in arrays]
        + [pltpu.SemaphoreType.DMA((len(arrays),))] * 2,
        compiler_params=pltpu.CompilerParams(vmem_limit_bytes=60 * 1024 * 1024),
        name="results",
    )(*arrays)


def shards(
    grad_out,
    expert_input,
    expert_index,
    route_weight,
    up_weight,
    down_weight,
    out_weight,
    *mixer_arrays,
):
    arrays = layer_part(
        grad_out,
        expert_input,
        expert_index,
        route_weight,
        up_weight[0],
        down_weight[0],
        out_weight,
        *mixer_arrays,
    )
    return results(*arrays)


def solution(mesh):
    in_specs = (
        P(("seq", "expert"), None),
        P(("seq", "expert"), None),
        P(("seq", "expert"), None),
        P(("seq", "expert"), None),
        P("expert", None, None),
        P("expert", None, None),
        P("expert", None),
        P("seq", "expert"),
        P(None, "expert"),
        P("expert", "seq"),
        P("expert", "seq"),
        P("expert"),
        P("seq", "expert"),
        P("seq", "expert"),
    )
    out_specs = (
        P(("seq", "expert"), None),
        P("seq", "expert"),
        P("seq", "expert"),
        P("seq", "expert"),
    )
    return jax.shard_map(shards, mesh=mesh, in_specs=in_specs, out_specs=out_specs, check_vma=False)
```

```python
import functools

import jax
import jax.numpy as jnp
from jax import lax
from jax.experimental import pallas as pl
from jax.experimental.pallas import tpu as pltpu
from jax.sharding import PartitionSpec as P

P_SIZE = 64
N = 128
KW = 4
SPAN = 128
LANES = 128
MESH = pl.DeviceIdType.MESH
F32 = jnp.float32
BF16 = jnp.bfloat16


def dot(a, b, left, right):
    return lax.dot_general(a, b, (((left,), (right,)), ((), ())), preferred_element_type=F32)


def widen(columns):
    lane = lax.broadcasted_iota(jnp.int32, (columns.shape[0], LANES), 1)
    parts = []
    for pair in range(columns.shape[1] // 2):
        one, two = columns[:, 2 * pair : 2 * pair + 1], columns[:, 2 * pair + 1 : 2 * pair + 2]
        parts.append(jnp.where(lane < P_SIZE, one, two))
    return jnp.concatenate(parts, axis=1)


def head_row(column, width):
    heads = column.shape[0]
    lane = lax.broadcasted_iota(jnp.int32, (heads, width), 1)
    head = lax.broadcasted_iota(jnp.int32, (heads, width), 0)
    chosen = jnp.where(lane // P_SIZE == head, column, 0.0)
    return jnp.broadcast_to(jnp.sum(chosen, axis=0, keepdims=True), (8, width))


def layer_kernel(
    input_ref,
    grad_ref,
    route_ref,
    up_ref,
    down_ref,
    out_weight_ref,
    value_hbm,
    in_basis_hbm,
    out_basis_hbm,
    taps_ref,
    step_ref,
    decay_ref,
    skip_ref,
    residual_ref,
    conv_ref,
    in_out_ref,
    out_out_ref,
    inputs,
    grads,
    partial,
    gathered,
    sibling_part,
    far_part,
    near_part,
    summed,
    routes,
    hidden,
    up,
    down,
    out_weight,
    out_grad,
    value_ref,
    in_basis_ref,
    out_basis_ref,
    mixed,
    weighted,
    grad_weighted,
    slope,
    masks,
    weights,
    in_part,
    out_part,
    value_grad,
    entering,
    leaving,
    running,
    edge,
    sum_rows,
    sum_columns,
    step_columns,
    scale_columns,
    grow_columns,
    block_row,
    prefix_row,
    suffix_row,
    tiles,
    landed,
    outs,
    returned,
    decay_tiles,
    decay_landed,
    halo,
    local_sem,
    send_sem,
    recv_sem,
    seq_send,
    seq_recv,
):
    here = lax.axis_index("seq")
    devices = lax.axis_size("seq")
    heads = step_ref.shape[0]
    blocks = step_ref.shape[1] // SPAN
    width = heads * P_SIZE
    length = blocks * SPAN
    strips = width // LANES
    depth = tiles.shape[2]

    me = lax.axis_index("expert")
    count = lax.axis_size("expert")
    chips = count // 2
    chip, core = me // 2, me % 2
    rows = input_ref.shape[0]
    half = rows // 2
    low, high, whole = pl.ds(0, half), pl.ds(half, half), pl.ds(0, rows)
    other, other_low, other_high = pl.ds(rows, rows), pl.ds(rows, half), pl.ds(rows + half, half)

    def device(chip_step, core_step):
        return ((chip + chip_step) % chips) * 2 + (core + core_step) % 2

    sibling, right, left = device(0, 1), device(1, 0), device(chips - 1, 0)
    copies = {}

    def send(name, source, target_ref, target):
        place = len(copies)
        copies[name] = pltpu.make_async_remote_copy(
            src_ref=source,
            dst_ref=target_ref,
            send_sem=send_sem.at[place],
            recv_sem=recv_sem.at[place],
            device_id={"expert": target},
            device_id_type=MESH,
        )
        copies[name].start()

    def arrived(*names):
        for name in names:
            copies[name].wait_recv()

    loads = []
    for place, (source, target) in enumerate(
        (
            (input_ref, inputs.at[0, whole]),
            (up_ref, up),
            (route_ref.at[me], routes.at[0]),
            (grad_ref, grads.at[0, whole]),
            (down_ref, down),
            (out_weight_ref, out_weight),
            (value_hbm, value_ref),
            (in_basis_hbm, in_basis_ref),
            (out_basis_hbm, out_basis_ref),
        )
    ):
        loads.append(pltpu.make_async_copy(source, target, local_sem.at[place]))
        loads[-1].start()

    barrier = pltpu.get_barrier_semaphore()
    for step in range(1, count):
        pl.semaphore_signal(
            barrier, inc=1, device_id={"expert": (me + step) % count}, device_id_type=MESH
        )

    def greet(step, carry):
        pl.semaphore_signal(
            barrier, inc=1, device_id={"seq": (here + step) % devices}, device_id_type=MESH
        )
        return carry

    lax.fori_loop(1, devices, greet, 0)
    pl.semaphore_wait(barrier, count + devices - 2)

    def first(tag, source, buffer):
        send(tag + "r1", source.at[low], buffer.at[1, low], right)
        send(tag + "l1", source.at[high], buffer.at[2, high], left)
        send(tag + "s0", source, buffer.at[0, other], sibling)

    def second(tag, source, buffer):
        send(tag + "r2", source.at[high], buffer.at[1, high], right)
        send(tag + "l2", source.at[low], buffer.at[2, low], left)

    def forward(tag, buffer):
        arrived(tag + "r1")
        send(tag + "r3", buffer.at[1, low], buffer.at[3, low], right)
        send(tag + "s1", buffer.at[1, low], buffer.at[1, other_low], sibling)
        arrived(tag + "l1")
        send(tag + "l3", buffer.at[2, high], buffer.at[3, high], left)
        send(tag + "s2", buffer.at[2, high], buffer.at[2, other_high], sibling)

    def share_near(tag, buffer):
        arrived(tag + "r2")
        send(tag + "s3", buffer.at[1, high], buffer.at[1, other_high], sibling)
        arrived(tag + "l2")
        send(tag + "s4", buffer.at[2, low], buffer.at[2, other_low], sibling)

    def share_far(tag, buffer):
        arrived(tag + "r3")
        send(tag + "s5", buffer.at[3, low], buffer.at[3, other_low], sibling)
        arrived(tag + "l3")
        send(tag + "s6", buffer.at[3, high], buffer.at[3, other_high], sibling)

    first("x", input_ref, inputs)
    first("g", grad_ref, grads)
    for chip_step, slot in ((0, 0), (1, 1), (chips - 1, 2), (2, 3)):
        for core_step in range(2):
            if (chip_step, core_step) != (0, 0):
                target = device(chip_step, core_step)
                send(
                    "w%d%d" % (slot, core_step),
                    route_ref.at[target],
                    routes.at[2 * slot + core_step],
                    target,
                )
    second("x", input_ref, inputs)

    lane = lax.broadcasted_iota(jnp.int32, (heads, SPAN), 1)
    ends = []
    for block in range(blocks):
        part = slice(block * SPAN, (block + 1) * SPAN)
        total = decay_ref[:, part]
        shift = 1
        while shift < SPAN:
            total = total + jnp.where(lane >= shift, pltpu.roll(total, shift, 1), 0.0)
            shift *= 2
        last = total[:, SPAN - 1 : SPAN]
        steps = step_ref[:, part]
        sum_rows[block] = total
        sum_columns[block] = total.T
        step_columns[block] = steps.T
        scale_columns[block] = (jnp.exp(last - total) * steps).T
        grow_columns[block] = jnp.exp(total).T
        block_row[block] = head_row(jnp.exp(last), width)
        ends.append(last)
    before = jnp.zeros((heads, 1), F32)
    after = jnp.zeros((heads, 1), F32)
    for block in range(blocks):
        prefix_row[block] = head_row(jnp.exp(before), width)
        before = before + ends[block]
        back = blocks - 1 - block
        suffix_row[back] = head_row(jnp.exp(after), width)
        after = after + ends[back]
    device_row = head_row(jnp.exp(before), width)
    for strip in range(strips):
        decay_tiles[strip] = device_row[:, strip * LANES : (strip + 1) * LANES]

    def rows_of(block):
        return pl.ds(pl.multiple_of(block * SPAN, SPAN), SPAN)

    def remote(place, source, target_ref, target):
        return pltpu.make_async_remote_copy(
            src_ref=source,
            dst_ref=target_ref,
            send_sem=seq_send.at[place],
            recv_sem=seq_recv.at[place],
            device_id={"seq": target},
            device_id_type=MESH,
        )

    def wait_all(place, sent, got):
        remote(place, sent, sent, (here + 1) % devices).wait_send()
        remote(place, got, got, (here + 1) % devices).wait_recv()

    rest = pl.ds(1, devices - 1)

    def scatter_state(way):
        for row in range(N // depth):
            for strip in range(strips):
                tiles[way, row * strips + strip] = running[
                    row * depth : (row + 1) * depth, strip * LANES : (strip + 1) * LANES
                ].astype(BF16)

        def one(step, carry):
            target = (here + step) % devices
            remote(way, tiles.at[way, target], landed.at[way, step], target).start()
            return carry

        lax.fori_loop(1, devices, one, 0)
        landed[way, 0] = tiles[way, here]

    def scan_state(way):
        wait_all(way, tiles.at[way, rest], landed.at[way, rest])
        state = jnp.zeros((depth, LANES), F32)

        def one(turn, state):
            place = turn if way == 0 else devices - 1 - turn
            slot = (here - place + devices) % devices
            outs[way, place] = state.astype(BF16)
            return decay_landed[slot][0:1] * state + landed[way, slot].astype(F32)

        lax.fori_loop(0, devices, one, state)

        def back(step, carry):
            target = (here + step) % devices
            remote(3 + way, outs.at[way, target], returned.at[way, here], target).start()
            return carry

        lax.fori_loop(1, devices, back, 0)
        returned[way, here] = outs[way, here]

    def collect_state(way):
        wait_all(3 + way, outs.at[way, rest], returned.at[way, rest])
        for row in range(N // depth):
            for strip in range(strips):
                edge[
                    way, row * depth : (row + 1) * depth, strip * LANES : (strip + 1) * LANES
                ] = returned[way, row * strips + strip].astype(F32)


    lane_row = lax.broadcasted_iota(jnp.int32, (1, LANES), 1)
    left_half = jnp.where(lane_row < P_SIZE, 1.0, 0.0).astype(BF16)
    right_half = jnp.where(lane_row < P_SIZE, 0.0, 1.0).astype(BF16)

    def weigh(block, carry):
        rows = rows_of(block)
        source = lax.broadcasted_iota(jnp.int32, (SPAN, SPAN), 0)
        reader = lax.broadcasted_iota(jnp.int32, (SPAN, SPAN), 1)
        lower = reader >= source
        scores = dot(in_basis_ref[rows], out_basis_ref[rows], 1, 1)
        for head in range(heads):
            gap = sum_rows[block, head : head + 1, :] - sum_columns[block][:, head : head + 1]
            mask = jnp.exp(jnp.where(lower, gap, -1e30)) * step_columns[block][:, head : head + 1]
            masks[block, head] = mask
            weights[block, :, head * SPAN : (head + 1) * SPAN] = (mask * scores).astype(BF16)
        return carry

    def local_start(block):
        rows = rows_of(block)
        scaled = (out_grad[rows].astype(F32) * widen(grow_columns[block])).astype(BF16)
        grad_weighted[rows] = scaled
        leaving[block] = dot(out_basis_ref[rows], scaled, 0, 0)

    def inside(block):
        rows = rows_of(block)
        in_basis, out_basis = in_basis_ref[rows], out_basis_ref[rows]
        total = jnp.zeros((SPAN, SPAN), F32)
        skip_row = widen(skip_ref[...])
        for strip in range(strips):
            span = slice(strip * LANES, (strip + 1) * LANES)
            grad_pair = out_grad[rows, span]
            act_pair = mixed[rows, span]
            act_two = jnp.concatenate([act_pair * left_half, act_pair * right_half], axis=0)
            grad_two = jnp.concatenate([grad_pair * left_half, grad_pair * right_half], axis=0)
            grad_mixed = dot(act_two, grad_pair, 1, 1)
            for side in range(2):
                total = total + masks[block, 2 * strip + side] * (
                    grad_mixed[side * SPAN : (side + 1) * SPAN]
                )
            pair = weights[block, :, 2 * strip * SPAN : 2 * (strip + 1) * SPAN]
            value_grad[rows, span] = dot(pair, grad_two, 1, 0) + skip_row[
                :, span
            ] * grad_pair.astype(F32)
        in_part[rows] = dot(total.astype(BF16), out_basis, 1, 0)
        out_part[rows] = dot(total.T.astype(BF16), in_basis, 1, 0)

    def chain_back():
        running[...] = jnp.zeros_like(running)

        def behind(turn, carry):
            block = blocks - 1 - turn
            added = leaving[block]
            leaving[block] = running[...]
            running[...] = block_row[block][0:1] * running[...] + added
            return carry

        lax.fori_loop(0, blocks, behind, 0)

    def close_out(block, carry):
        rows = rows_of(block)
        enter = (entering[block] + prefix_row[block][0:1] * edge[0]).astype(BF16)
        out_out_ref[rows] = (out_part[rows] + dot(grad_weighted[rows], enter, 1, 1)).astype(BF16)
        return carry

    def close(block, carry):
        rows = rows_of(block)
        leave = (leaving[block] + suffix_row[block][0:1] * edge[1]).astype(BF16)
        carried = dot(in_basis_ref[rows], leave, 1, 0)
        value_grad[rows] = (value_grad[rows] + widen(scale_columns[block]) * carried) * slope[rows]
        in_out_ref[rows] = (in_part[rows] + dot(weighted[rows], leave, 1, 1)).astype(BF16)
        return carry

    def inner_blocks(chip_step, work):
        def one(core_step, carry):
            work(device(chip_step, core_step))
            return carry

        lax.fori_loop(0, 2, one, 0)

    def both(block):
        local_start(block)
        inside(block)

    def before(slot):
        hidden[slot] = 2.0 * jnp.maximum(dot(inputs[slot], up[...], 1, 0), 0.0)

    def after(slot):
        column = jnp.concatenate(
            [routes[2 * slot].T[:, 0:1], routes[2 * slot + 1].T[:, 0:1]], axis=0
        )
        back = dot(grads[slot], down[...], 1, 1) * column
        inner = (hidden[slot] * back).astype(BF16)
        partial[slot] = dot(inner, up[...], 1, 1).astype(BF16)
        send("p%d" % slot, partial.at[slot, other], sibling_part.at[slot], sibling)

    def after_half(slot, part, other_part, tag):
        column = jnp.concatenate(
            [routes[2 * slot].T[part.start : part.start + half, 0:1]]
            + [routes[2 * slot + 1].T[part.start : part.start + half, 0:1]],
            axis=0,
        )
        both_grads = jnp.concatenate([grads[slot, part], grads[slot, other_part]], axis=0)
        both_hidden = jnp.concatenate([hidden[slot, part], hidden[slot, other_part]], axis=0)
        back = dot(both_grads, down[...], 1, 1) * column
        inner = (both_hidden * back).astype(BF16)
        product = dot(inner, up[...], 1, 1).astype(BF16)
        partial[slot, part] = product[0:half]
        partial[slot, other_part] = product[half : 2 * half]
        send(tag, partial.at[slot, other_part], sibling_part.at[slot, part], sibling)

    loads[0].wait()
    loads[1].wait()
    arrived("xs0")
    before(0)
    forward("x", inputs)
    for place in (6, 7, 8):
        loads[place].wait()
    running[...] = jnp.zeros_like(running)

    def ahead(block, carry):
        rows = rows_of(block)
        value = value_ref[rows].astype(F32)
        sigmoid = jax.nn.sigmoid(value)
        act = (value * sigmoid).astype(BF16)
        mixed[rows] = act
        slope[rows] = sigmoid + value * sigmoid * (1.0 - sigmoid)
        scaled = (act.astype(F32) * widen(scale_columns[block])).astype(BF16)
        weighted[rows] = scaled
        entering[block] = running[...]
        running[...] = block_row[block][0:1] * running[...] + dot(in_basis_ref[rows], scaled, 0, 0)
        return carry

    lax.fori_loop(0, blocks, ahead, 0)

    def send_decay(step, carry):
        target = (here + step) % devices
        remote(2, decay_tiles.at[target % strips], decay_landed.at[step], target).start()
        return carry

    lax.fori_loop(1, devices, send_decay, 0)
    decay_landed[0] = decay_tiles[here % strips]
    scatter_state(0)

    loads[2].wait()
    for slot, core_step in ((0, 1), (1, 0), (1, 1), (2, 0), (2, 1), (3, 0), (3, 1)):
        arrived("w%d%d" % (slot, core_step))
    loads[3].wait()
    loads[4].wait()
    forward("g", grads)
    second("g", grad_ref, grads)
    arrived("gs0")
    after(0)
    lax.fori_loop(0, blocks, weigh, 0)
    share_near("x", inputs)
    arrived("xs1", "xs3")
    before(1)
    arrived("xs2", "xs4")
    before(2)
    arrived("gs1")
    after_half(1, low, other_low, "p1low")
    arrived("gs2")
    after_half(2, high, other_high, "p2high")
    share_far("x", inputs)
    arrived("xs5", "xs6")
    before(3)
    wait_all(2, decay_landed.at[rest], decay_landed.at[rest])
    scan_state(0)
    share_far("g", grads)
    arrived("gs5", "gs6")
    after(3)
    arrived("p3")
    summed[0] = partial[3, whole] + sibling_part[3]
    send("fr", summed.at[0, low], far_part.at[0], right)
    send("fl", summed.at[0, high], far_part.at[1], left)
    arrived("p2high")
    summed[1, high] = partial[2, high] + sibling_part[2, high]
    send("nr1", summed.at[1, high], near_part.at[0, high], right)
    arrived("p1low")
    summed[2, low] = partial[1, low] + sibling_part[1, low]
    send("nl1", summed.at[2, low], near_part.at[1, low], left)
    share_near("g", grads)
    arrived("gs4")
    after_half(2, low, other_low, "p2low")
    arrived("gs3")
    after_half(1, high, other_high, "p1high")

    def three(a, b, c):
        return (a.astype(F32) + b.astype(F32) + c.astype(F32)).astype(BF16)

    arrived("fr", "p2low")
    summed[1, low] = three(partial[2, low], sibling_part[2, low], far_part[0])
    send("nr2", summed.at[1, low], near_part.at[0, low], right)
    arrived("fl", "p1high")
    summed[2, high] = three(partial[1, high], sibling_part[1, high], far_part[1])
    send("nl2", summed.at[2, high], near_part.at[1, high], left)
    loads[5].wait()
    arrived("p0")

    def finish(part):
        gathered[0, part] = (
            grads[0, part].astype(F32)
            + partial[0, part].astype(F32)
            + sibling_part[0, part].astype(F32)
            + near_part[0, part].astype(F32)
            + near_part[1, part].astype(F32)
        ).astype(BF16)

    own = gathered.at[0, whole]
    arrived("nl1", "nr2")
    finish(low)
    send("or1", own.at[low], gathered.at[1, low], right)
    arrived("nr1", "nl2")
    finish(high)
    send("ol1", own.at[high], gathered.at[2, high], left)
    send("os0", own, gathered.at[0, other], sibling)
    second("o", own, gathered)
    store = pltpu.make_async_copy(own, residual_ref, local_sem.at[0])
    store.start()

    def project(slot, chip_step):
        product = dot(gathered[slot], out_weight[...], 1, 1).astype(BF16)
        for core_step in range(2):
            start = pl.multiple_of(device(chip_step, core_step) * rows, rows)
            out_grad[pl.ds(start, rows)] = product[core_step * rows : (core_step + 1) * rows]

    arrived("os0")
    project(0, 0)
    inner_blocks(0, both)
    forward("o", gathered)
    share_near("o", gathered)
    arrived("os1", "os3")
    project(1, chips - 1)
    inner_blocks(chips - 1, both)
    arrived("os2", "os4")
    project(2, 1)
    inner_blocks(1, both)
    share_far("o", gathered)
    arrived("os5", "os6")
    project(3, 2)
    inner_blocks(2, local_start)
    chain_back()
    scatter_state(1)
    inner_blocks(2, inside)
    scan_state(1)
    collect_state(0)
    lax.fori_loop(0, blocks, close_out, 0)
    collect_state(1)
    close(0, 0)
    ahead_rows = remote(5, value_grad.at[pl.ds(0, 8)], halo, (here + devices - 1) % devices)
    ahead_rows.start()
    lax.fori_loop(1, blocks, close, 0)
    ahead_rows.wait()
    value_grad[pl.ds(length, 8)] = jnp.where(here == devices - 1, 0.0, halo[...])

    def filtered(block, carry):
        start = pl.multiple_of(block * SPAN, SPAN)
        window = value_grad[pl.ds(start, SPAN + 8)]
        summed = taps_ref[0:1] * window[0:SPAN]
        for tap in range(1, KW):
            summed = summed + taps_ref[tap : tap + 1] * window[tap : tap + SPAN]
        conv_ref[pl.ds(start, SPAN)] = summed.astype(BF16)
        return carry

    lax.fori_loop(0, blocks, filtered, 0)


    store.wait()
    for copy in copies.values():
        copy.wait_send()


def layer_part(
    grad_out,
    expert_input,
    expert_index,
    route_weight,
    up,
    down,
    out_weight,
    value,
    taps,
    step,
    decay,
    skip,
    in_basis,
    out_basis,
):
    count = lax.axis_size("expert")
    rows, wide = grad_out.shape
    inner = up.shape[1]
    match = expert_index[None] == jnp.arange(count, dtype=jnp.int32)[:, None, None]
    table = jnp.sum(jnp.where(match, route_weight[None], 0.0), axis=2)
    routes = jnp.broadcast_to(table[:, None, :], (count, 8, rows))
    copies = 64
    devices = lax.axis_size("seq")
    heads, length = step.shape
    blocks = length // SPAN
    width = heads * P_SIZE
    strips = width // LANES
    depth = N * strips // devices
    hbm = pl.BlockSpec(memory_space=pl.ANY)
    vmem = pl.BlockSpec(memory_space=pltpu.VMEM)
    return pl.pallas_call(
        layer_kernel,
        out_shape=(
            jax.ShapeDtypeStruct((rows, wide), BF16),
            jax.ShapeDtypeStruct((length, width), BF16),
            jax.ShapeDtypeStruct((length, N), BF16),
            jax.ShapeDtypeStruct((length, N), BF16),
        ),
        in_specs=[hbm] * 9 + [vmem] * 4,
        out_specs=(hbm, vmem, vmem, vmem),
        scratch_shapes=[
            pltpu.VMEM((4, 2 * rows, wide), BF16),
            pltpu.VMEM((4, 2 * rows, wide), BF16),
            pltpu.VMEM((4, 2 * rows, wide), BF16),
            pltpu.VMEM((4, 2 * rows, wide), BF16),
            pltpu.VMEM((4, rows, wide), BF16),
            pltpu.VMEM((2, rows // 2, wide), BF16),
            pltpu.VMEM((2, rows, wide), BF16),
            pltpu.VMEM((3, rows, wide), BF16),
            pltpu.VMEM((8, 8, rows), F32),
            pltpu.VMEM((4, 2 * rows, inner), F32),
            pltpu.VMEM((wide, inner), BF16),
            pltpu.VMEM((inner, wide), BF16),
            pltpu.VMEM((width, wide), BF16),
            pltpu.VMEM((length, width), BF16),
            pltpu.VMEM((length, width), BF16),
            pltpu.VMEM((length, N), BF16),
            pltpu.VMEM((length, N), BF16),
            pltpu.VMEM((length, width), BF16),
            pltpu.VMEM((length, width), BF16),
            pltpu.VMEM((length, width), BF16),
            pltpu.VMEM((length, width), F32),
            pltpu.VMEM((blocks, heads, SPAN, SPAN), F32),
            pltpu.VMEM((blocks, SPAN, heads * SPAN), BF16),
            pltpu.VMEM((length, N), F32),
            pltpu.VMEM((length, N), F32),
            pltpu.VMEM((length + 8, width), F32),
            pltpu.VMEM((blocks, N, width), F32),
            pltpu.VMEM((blocks, N, width), F32),
            pltpu.VMEM((N, width), F32),
            pltpu.VMEM((2, N, width), F32),
            pltpu.VMEM((blocks, heads, SPAN), F32),
            pltpu.VMEM((blocks, SPAN, heads), F32),
            pltpu.VMEM((blocks, SPAN, heads), F32),
            pltpu.VMEM((blocks, SPAN, heads), F32),
            pltpu.VMEM((blocks, SPAN, heads), F32),
            pltpu.VMEM((blocks, 8, width), F32),
            pltpu.VMEM((blocks, 8, width), F32),
            pltpu.VMEM((blocks, 8, width), F32),
            pltpu.VMEM((2, devices, depth, LANES), BF16),
            pltpu.VMEM((2, devices, depth, LANES), BF16),
            pltpu.VMEM((2, devices, depth, LANES), BF16),
            pltpu.VMEM((2, devices, depth, LANES), BF16),
            pltpu.VMEM((strips, 8, LANES), F32),
            pltpu.VMEM((devices, 8, LANES), F32),
            pltpu.VMEM((8, width), F32),
            pltpu.SemaphoreType.DMA((9,)),
            pltpu.SemaphoreType.DMA((copies,)),
            pltpu.SemaphoreType.DMA((copies,)),
            pltpu.SemaphoreType.DMA((6,)),
            pltpu.SemaphoreType.DMA((6,)),
        ],
        compiler_params=pltpu.CompilerParams(
            collective_id=1, has_side_effects=True, vmem_limit_bytes=67043328
        ),
        name="layer_part",
    )(
        expert_input,
        grad_out,
        routes,
        up,
        down,
        out_weight,
        value,
        in_basis,
        out_basis,
        taps,
        step,
        decay,
        skip[None],
    )


def results_kernel(*refs):
    sources, targets, held, (in_sem, out_sem) = refs[0:4], refs[4:8], refs[8:12], refs[12:14]
    loads, stores = [], []
    for place in range(4):
        loads.append(pltpu.make_async_copy(sources[place], held[place], in_sem.at[place]))
        loads[-1].start()
    for place in range(4):
        loads[place].wait()
        stores.append(pltpu.make_async_copy(held[place], targets[place], out_sem.at[place]))
        stores[-1].start()
    for store in stores:
        store.wait()


def results(*arrays):
    shapes = [jax.ShapeDtypeStruct(array.shape, array.dtype) for array in arrays]
    hbm = pl.BlockSpec(memory_space=pl.ANY)
    return pl.pallas_call(
        results_kernel,
        out_shape=tuple(shapes),
        in_specs=[hbm] * len(arrays),
        out_specs=(hbm,) * len(arrays),
        scratch_shapes=[pltpu.VMEM(array.shape, array.dtype) for array in arrays]
        + [pltpu.SemaphoreType.DMA((len(arrays),))] * 2,
        compiler_params=pltpu.CompilerParams(vmem_limit_bytes=60 * 1024 * 1024),
        name="results",
    )(*arrays)


def shards(
    grad_out,
    expert_input,
    expert_index,
    route_weight,
    up_weight,
    down_weight,
    out_weight,
    *mixer_arrays,
):
    arrays = layer_part(
        grad_out,
        expert_input,
        expert_index,
        route_weight,
        up_weight[0],
        down_weight[0],
        out_weight,
        *mixer_arrays,
    )
    return results(*arrays)


def solution(mesh):
    in_specs = (
        P(("seq", "expert"), None),
        P(("seq", "expert"), None),
        P(("seq", "expert"), None),
        P(("seq", "expert"), None),
        P("expert", None, None),
        P("expert", None, None),
        P("expert", None),
        P("seq", "expert"),
        P(None, "expert"),
        P("expert", "seq"),
        P("expert", "seq"),
        P("expert"),
        P("seq", "expert"),
        P("seq", "expert"),
    )
    out_specs = (
        P(("seq", "expert"), None),
        P("seq", "expert"),
        P("seq", "expert"),
        P("seq", "expert"),
    )
    return jax.shard_map(shards, mesh=mesh, in_specs=in_specs, out_specs=out_specs, check_vma=False)
```
